128 devices in a mesh: tm: 64 (over z, y, x), cells: 2 (over core).
Axes of the slice: x: 4, y: 4, z: 4, core: 2. Of those that a mesh axis runs over, the one named last changes fastest.
Arguments:
- flux: bfloat16 [64, 512, 8192], P(None, 'tm', 'cells'), may hold values from -6 to 6
- footprint: bfloat16 [16384, 4, 8192], P('tm', None, 'cells'), may hold values from -0.046875 to 0.046875
- band_lag: int32 [16384, 4], P('tm'), may hold values from 0 to 23, as said below
- obs_hour: int32 [16384], P('tm'), may hold values from 0 to 511, as said below
- tile_mask: int32 [16384, 64], P('tm', 'cells'), may hold values 0 or 1
- obs_value: float32 [64, 16384], P(None, 'tm'), may hold values from -6 to 6
- obs_weight: float32 [16384], P('tm'), may hold values from 4 to 64
Outputs:
- modeled: float32 [64, 16384], P(None, 'tm')
- gradient: float32 [64, 512, 8192], P(None, 'tm', 'cells')
The draws below stay inside these ranges and needn't reach their ends.
Inputs may be any that keep to these rules, and one draw needn't show every extreme that they name: `band_lag`: each row holds 4 different lags. `obs_hour`: observation i has an hour in [(i // 256) * 8, (i // 256 + 1) * 8).
All inputs are finite; a program needn't handle non-finite values. No bound on the sum of `tile_mask` on one device may be relied on, other than what follows from the above.
Results may differ from the reference program's by a relative error of at most 0.0029.
Values may be sent and summed in bfloat16 or wider, within the bound.
No kernel may reach another device: no remote copies, remote signals or barrier semaphores. Data moves between devices by JAX's collectives and lax.ppermute only.
A program may use at most 320 MiB of HBM per device.

```python
import math
import jax
import jax.numpy as jnp
from jax import lax

LAGS = 24
BANDS = 4
HOURS_DEV = 8
TILE = 128
OBS_DEV = 256
SAMPLES = 64
HOURS = 512
OBS = 16384
CELLS = 8192
TILES = 64


def draw_band_lag(key, part):
    scores = jax.random.randint(jax.random.fold_in(key, 11), (OBS, LAGS), 0, 1048576)
    scores = scores * LAGS + jnp.arange(LAGS, dtype=jnp.int32)[None, :]
    ordering = jnp.argsort(scores, axis=1, stable=True)
    return ordering[:, :BANDS].astype(jnp.int32)


def draw_obs_hour(key, part):
    owner = jnp.arange(OBS, dtype=jnp.int32) // OBS_DEV
    within = jax.random.randint(jax.random.fold_in(key, 23), (OBS,), 0, HOURS_DEV)
    return (owner * HOURS_DEV + within).astype(jnp.int32)


def with_ends(entries, rng, least, top_value):
    longest = entries.shape.index(max(entries.shape))
    spots = []
    for shift in (0, 1):
        where = [jax.random.randint(jax.random.fold_in(rng, axis), (), 0, length) for axis, length in enumerate(entries.shape)]
        where[longest] = (where[longest] + shift) % entries.shape[longest]
        spots.append(tuple(where))
    return entries.at[spots[0]].set(least).at[spots[1]].set(top_value)


def block_levels(rng, shape, cuts, low, top_value):
    level, own = 1.0, jax.random.fold_in(rng, 6)
    for position, blocks in cuts:
        heights = jnp.exp(jax.random.uniform(jax.random.fold_in(own, position), (blocks,), jnp.float32, low / len(cuts), top_value / len(cuts)))
        level = level * jnp.repeat(heights, shape[position] // blocks).reshape([-1 if axis == position else 1 for axis in range(len(shape))])
    return level


def scatter_about(stream_key, extent, deviation, most, cuts=(), kind=jnp.bfloat16):
    result = jax.random.normal(stream_key, extent, jnp.float32) * deviation
    if len(cuts) > 0:
        result = block_levels(stream_key, extent, cuts, -0.22, 0.18) * result
    return jnp.clip(result, min=-most, max=most).astype(kind)


def setup_inputs(seed: int = 0) -> dict:
    key_list = jax.random.split(jax.random.key(seed), 8)
    flux = scatter_about(key_list[0], (SAMPLES, HOURS, CELLS), 1.0, 6.0, ((1, 64), (2, 2)))
    footprint = scatter_about(key_list[1], (OBS, BANDS, CELLS), (BANDS * CELLS // 2) ** -0.5, 0.046875, ((0, 64), (2, 2)))
    band_lag = draw_band_lag(jax.random.fold_in(key_list[7], 71), 0)
    obs_hour = draw_obs_hour(jax.random.fold_in(key_list[7], 71), 0)
    tile_mask = with_ends((jax.random.randint(key_list[4], (OBS, TILES), 0, 2) < 1).astype(jnp.int32), jax.random.fold_in(key_list[4], 1), 0, 1)
    obs_value = scatter_about(key_list[5], (SAMPLES, OBS), 1.0, 6.0, ((1, 64),), jnp.float32)
    obs_weight = jnp.clip(jnp.exp(math.log(64.0) - 2.7725887 * jax.random.uniform(key_list[6], (OBS,), jnp.float32) ** block_levels(key_list[6], (OBS,), ((0, 64),), -0.2, 0.2)), 4.0, 64.0)
    return {"flux": flux, "footprint": footprint, "band_lag": band_lag, "obs_hour": obs_hour, "tile_mask": tile_mask, "obs_value": obs_value, "obs_weight": obs_weight}


def reference(flux, footprint, band_lag, obs_hour, tile_mask, obs_value, obs_weight):
    group_rows = 8
    groups = OBS // group_rows
    source = obs_hour[:, None] - band_lag
    in_range = (source >= 0).astype(jnp.float32)
    hour_index = jnp.maximum(source, 0).astype(jnp.int32)

    def weights_of(prints, tiles_on, inside):
        spread = jnp.repeat(tiles_on.astype(jnp.float32), TILE, axis=1)
        return prints.astype(jnp.float32) * spread[:, None, :] * inside[:, :, None]

    grouped = (footprint.reshape(groups, group_rows, BANDS, CELLS),
               tile_mask.reshape(groups, group_rows, TILES),
               in_range.reshape(groups, group_rows, BANDS),
               hour_index.reshape(groups, group_rows, BANDS))

    def forward(inputs):
        prints, tiles_on, inside, hours_at = inputs
        weighted = weights_of(prints, tiles_on, inside)
        picked = jnp.take(flux, hours_at.reshape(-1), axis=1).astype(jnp.float32)
        picked = picked.reshape(SAMPLES, group_rows, BANDS, CELLS)
        return jnp.einsum('sobc,obc->so', picked, weighted, precision=lax.Precision.HIGHEST)

    modeled = lax.map(forward, grouped)
    modeled = jnp.transpose(modeled, (1, 0, 2)).reshape(SAMPLES, OBS)
    residual = (obs_weight[None, :] * (modeled - obs_value)).astype(jnp.bfloat16)
    misfit = jnp.transpose(residual.astype(jnp.float32).reshape(SAMPLES, groups, group_rows), (1, 0, 2))

    def adjoint(accumulated, inputs):
        prints, tiles_on, inside, hours_at, weighted_res = inputs
        weighted = weights_of(prints, tiles_on, inside)
        contrib = jnp.einsum('so,obc->sobc', weighted_res, weighted, precision=lax.Precision.HIGHEST)
        contrib = contrib.reshape(SAMPLES, group_rows * BANDS, CELLS)
        accumulated = accumulated.at[:, hours_at.reshape(-1), :].add(contrib)
        return accumulated, None

    gradient, _ = lax.scan(adjoint, jnp.zeros((SAMPLES, HOURS, CELLS), jnp.float32), grouped + (misfit,))
    return modeled, gradient
```

```python
import functools

import jax
import jax.numpy as jnp
from jax import lax
from jax.experimental import pallas as pl
from jax.experimental.pallas import tpu as pltpu
from jax.sharding import PartitionSpec as P

REACH = 3
TILE = 128
STEP_TILES = 8
ROUND_ROWS = (256, 256, 128)
VMEM_BYTES = 40 * 1024 * 1024


def shifted(value, steps):
    count = lax.axis_size("tm")
    initial, last = (max(0, -steps), min(count, count - steps))
    return lax.ppermute(value, "tm", [(source, source + steps) for source in range(initial, last)])


def swapped(value):
    return lax.ppermute(value, "cells", [(0, 1), (1, 0)])


def one_hot(wanted, position):
    return jnp.where(wanted == position, 1.0, 0.0).astype(jnp.bfloat16)


def pack_body(place_ref, prints_ref, *out_refs):
    rows = prints_ref.shape[0]
    for tile in range(STEP_TILES):
        cells = slice(tile * TILE, (tile + 1) * TILE)
        prints = prints_ref[:, cells]
        for lag, out_ref in enumerate(out_refs):
            place = place_ref[lag, tile : tile + 1, :]
            slots = lax.broadcasted_iota(jnp.int32, (out_ref.shape[0], rows), 0)
            moved = jnp.dot(one_hot(slots, place), prints, preferred_element_type=jnp.float32)
            out_ref[:, cells] = moved.astype(jnp.bfloat16)


def pack(place, prints):
    rows, cells = prints.shape
    width = STEP_TILES * TILE
    return pl.pallas_call(
        pack_body,
        grid=(cells // width,),
        in_specs=[
            pl.BlockSpec((REACH, STEP_TILES, rows), lambda step: (0, step, 0)),
            pl.BlockSpec((rows, width), lambda step: (0, step)),
        ],
        out_specs=[pl.BlockSpec((room, width), lambda step: (0, step)) for room in ROUND_ROWS],
        out_shape=[jax.ShapeDtypeStruct((room, cells), jnp.bfloat16) for room in ROUND_ROWS],
        compiler_params=pltpu.CompilerParams(vmem_limit_bytes=VMEM_BYTES),
        cost_estimate=pl.CostEstimate(
            flops=2 * sum(ROUND_ROWS) * rows * cells, bytes_accessed=4 * rows * cells, transcendentals=0
        ),
        name="pack",
    )(place, prints)


def add_products(flux_ref, prints_ref, sums_ref):
    bands, _, obs = sums_ref.shape

    def one_band(band, carry):
        part = prints_ref[pl.ds(pl.multiple_of(band * obs, obs), obs), :]
        sums_ref[band] += lax.dot_general(
            flux_ref[...], part, (((1,), (1,)), ((), ())), preferred_element_type=jnp.float32
        )
        return carry

    lax.fori_loop(0, bands, one_band, 0)


def finish_products(hour_ref, out_ref, sums_ref):
    bands, samples_hours, obs = sums_ref.shape
    samples = out_ref.shape[0]
    hours = samples_hours // samples
    row_hour = lax.rem(lax.broadcasted_iota(jnp.int32, (samples_hours, obs), 0), hours)
    total = jnp.zeros((samples_hours, obs), jnp.float32)
    for band in range(bands):
        total = total + jnp.where(hour_ref[band : band + 1, :] == row_hour, sums_ref[band], 0.0)
    out_ref[...] = jnp.sum(total.reshape(samples, hours, obs), axis=1)


def own_body(flux_ref, prints_ref, hour_ref, out_ref, sums_ref):
    step = pl.program_id(0)

    @pl.when(step == 0)
    def _():
        sums_ref[...] = jnp.zeros_like(sums_ref)

    add_products(flux_ref, prints_ref, sums_ref)

    @pl.when(step == pl.num_programs(0) - 1)
    def _():
        finish_products(hour_ref, out_ref, sums_ref)


def own_products(flux, prints, hour_of, samples):
    rows, cells = prints.shape
    bands, obs = hour_of.shape
    width = STEP_TILES * TILE
    return pl.pallas_call(
        own_body,
        grid=(cells // width,),
        in_specs=[
            pl.BlockSpec((flux.shape[0], width), lambda step: (0, step)),
            pl.BlockSpec((rows, width), lambda step: (0, step)),
            pl.BlockSpec((bands, obs), lambda step: (0, 0)),
        ],
        out_specs=pl.BlockSpec((samples, obs), lambda step: (0, 0)),
        out_shape=jax.ShapeDtypeStruct((samples, obs), jnp.float32),
        scratch_shapes=[pltpu.VMEM((bands, flux.shape[0], obs), jnp.float32)],
        compiler_params=pltpu.CompilerParams(vmem_limit_bytes=VMEM_BYTES),
        cost_estimate=pl.CostEstimate(
            flops=2 * flux.shape[0] * rows * cells, bytes_accessed=3 * rows * cells, transcendentals=0
        ),
        name="own_products",
    )(flux, prints, hour_of)


def unpack_body(flux_ref, moved_ref, place_ref, hour_ref, prints_ref, out_ref, sums_ref):
    step = pl.program_id(0)
    rows, room = prints_ref.shape[0], moved_ref.shape[0]

    @pl.when(step == 0)
    def _():
        sums_ref[...] = jnp.zeros_like(sums_ref)

    for tile in range(STEP_TILES):
        cells = slice(tile * TILE, (tile + 1) * TILE)
        place = place_ref[0, :, tile : tile + 1]
        slots = lax.broadcasted_iota(jnp.int32, (rows, room), 1)
        back = jnp.dot(one_hot(slots, place), moved_ref[:, cells], preferred_element_type=jnp.float32)
        prints_ref[:, cells] = back.astype(jnp.bfloat16)
    add_products(flux_ref, prints_ref, sums_ref)

    @pl.when(step == pl.num_programs(0) - 1)
    def _():
        finish_products(hour_ref, out_ref, sums_ref)


def unpack_products(flux, moved, place, hour_of, samples):
    steps, rows, _ = place.shape
    room, cells = moved.shape
    bands, obs = hour_of.shape
    width = STEP_TILES * TILE
    return pl.pallas_call(
        unpack_body,
        grid=(steps,),
        in_specs=[
            pl.BlockSpec((flux.shape[0], width), lambda step: (0, step)),
            pl.BlockSpec((room, width), lambda step: (0, step)),
            pl.BlockSpec((1, rows, STEP_TILES), lambda step: (step, 0, 0)),
            pl.BlockSpec((bands, obs), lambda step: (0, 0)),
        ],
        out_specs=[
            pl.BlockSpec((rows, width), lambda step: (0, step)),
            pl.BlockSpec((samples, obs), lambda step: (0, 0)),
        ],
        out_shape=[
            jax.ShapeDtypeStruct((rows, cells), jnp.bfloat16),
            jax.ShapeDtypeStruct((samples, obs), jnp.float32),
        ],
        scratch_shapes=[pltpu.VMEM((bands, flux.shape[0], obs), jnp.float32)],
        compiler_params=pltpu.CompilerParams(vmem_limit_bytes=VMEM_BYTES),
        cost_estimate=pl.CostEstimate(
            flops=2 * (flux.shape[0] + room) * rows * cells, bytes_accessed=5 * rows * cells, transcendentals=0
        ),
        name="unpack_products",
    )(flux, moved, place, hour_of)


def adjoint_body(*refs):
    count = REACH + 1
    residual_refs, hour_refs, prints_refs = refs[:count], refs[count : 2 * count], refs[2 * count : 3 * count]
    out_ref, spread_ref = refs[3 * count :]
    bands, samples_hours, obs = spread_ref.shape[1:]
    samples = residual_refs[0].shape[0]
    hours = samples_hours // samples

    @pl.when(pl.program_id(0) == 0)
    def _():
        row_hour = lax.broadcasted_iota(jnp.int32, (samples, hours, obs), 1)
        for lag in range(count):
            value = residual_refs[lag][...].astype(jnp.float32)
            value = jnp.broadcast_to(value[:, None, :], (samples, hours, obs))
            for band in range(bands):
                wanted = hour_refs[lag][band : band + 1, :][None]
                spread = jnp.where(wanted == row_hour, value, 0.0).reshape(samples_hours, obs)
                spread_ref[lag, band] = spread.astype(jnp.bfloat16)

    total = jnp.zeros(out_ref.shape, jnp.float32)
    for lag in range(count):
        for band in range(bands):
            part = prints_refs[lag][band * obs : (band + 1) * obs, :]
            total = total + jnp.dot(spread_ref[lag, band], part, preferred_element_type=jnp.float32)
    out_ref[...] = total


def adjoint(residuals, hours_of, prints, samples_hours, width=256):
    rows, cells = prints[0].shape
    bands, obs = hours_of[0].shape
    count = REACH + 1
    whole = lambda step: (0, 0)
    return pl.pallas_call(
        adjoint_body,
        grid=(cells // width,),
        in_specs=[pl.BlockSpec(residuals[0].shape, whole)] * count
        + [pl.BlockSpec((bands, obs), whole)] * count
        + [pl.BlockSpec((rows, width), lambda step: (0, step))] * count,
        out_specs=pl.BlockSpec((samples_hours, width), lambda step: (0, step)),
        out_shape=jax.ShapeDtypeStruct((samples_hours, cells), jnp.float32),
        scratch_shapes=[pltpu.VMEM((count, bands, samples_hours, obs), jnp.bfloat16)],
        compiler_params=pltpu.CompilerParams(vmem_limit_bytes=VMEM_BYTES),
        cost_estimate=pl.CostEstimate(
            flops=2 * count * samples_hours * rows * cells, bytes_accessed=10 * rows * cells, transcendentals=0
        ),
        name="adjoint",
    )(*residuals, *hours_of, *prints)


def body(flux, footprint, band_lag, obs_hour, tile_mask, obs_value, obs_weight):
    samples, hours, cells = flux.shape
    obs, bands, _ = footprint.shape
    tiles = tile_mask.shape[1]
    rows = bands * obs
    position = lax.axis_index("tm")
    flux_rows = flux.reshape(samples * hours, cells)

    source = (obs_hour[:, None] - band_lag).T
    mask = tile_mask.T
    note = jnp.concatenate([mask, source, jnp.zeros((8 - bands, obs), jnp.int32)], axis=0)
    notes = [shifted(note, -lag) for lag in range(1, REACH + 1)]

    def hour_in(hour, block):
        inside = hour - block * hours
        return jnp.where((inside >= 0) & (inside < hours), inside, -1)

    def wanted(hour_of, tile_on):
        return jnp.tile(tile_on, (1, bands)) * (hour_of.reshape(1, rows) >= 0).astype(jnp.int32)

    keep = jnp.repeat(tile_mask.astype(jnp.bfloat16), cells // tiles, axis=1)
    prints = (footprint * keep[:, None, :]).transpose(1, 0, 2).reshape(rows, cells)

    ahead = lax.broadcasted_iota(jnp.int32, (rows, rows), 0) < lax.broadcasted_iota(jnp.int32, (rows, rows), 1)
    ahead = ahead.astype(jnp.bfloat16)

    leaving = jnp.stack([wanted(hour_in(source, position - lag), mask) for lag in range(1, REACH + 1)])
    counts = jnp.max(jnp.sum(leaving, axis=2), axis=1)
    place = lax.dot_general(
        leaving.astype(jnp.bfloat16), ahead, (((2,), (0,)), ((), ())), preferred_element_type=jnp.float32
    )
    place = jnp.where(leaving > 0, place.astype(jnp.int32), -1)
    room = jnp.array(ROUND_ROWS, jnp.int32)
    rounds = lax.pmax(jnp.max((counts + room - 1) // room), ("tm", "cells"))

    hours_of, arrived = [], []
    for lag in range(1, REACH + 1):
        their_mask, their_source = notes[lag - 1][:tiles], notes[lag - 1][tiles : tiles + bands]
        hour_of = hour_in(their_source, position)
        coming = wanted(hour_of, their_mask)
        order = lax.dot_general(
            ahead, coming.astype(jnp.bfloat16), (((0,), (1,)), ((), ())), preferred_element_type=jnp.float32
        )
        order = jnp.where(coming.T > 0, order.astype(jnp.int32), -1)
        hours_of.append(hour_of)
        arrived.append(order.reshape(rows, tiles // STEP_TILES, STEP_TILES).transpose(1, 0, 2))

    def one_round(index):
        packed = pack(place - (index * room)[:, None, None], prints)
        moved = [shifted(packed[lag - 1], -lag) for lag in range(1, REACH + 1)]
        return [
            unpack_products(flux_rows, moved[lag], arrived[lag] - index * room[lag], hours_of[lag], samples)
            for lag in range(REACH)
        ]

    own_hours = hour_in(source, position)
    own = own_products(flux_rows, prints, own_hours, samples)
    first = one_round(0)

    def further(index, state):
        more = one_round(index)
        return [(a + c, b + d) for (a, b), (c, d) in zip(state, more)]

    gathered = lax.fori_loop(1, rounds, further, [tuple(pair) for pair in first])

    partial = own
    for lag in range(1, REACH + 1):
        partial = partial + shifted(gathered[lag - 1][1], lag)
    modeled = partial + swapped(partial)
    residual = (obs_weight[None, :] * (modeled - obs_value)).astype(jnp.bfloat16)
    residuals = [residual] + [shifted(residual, -lag) for lag in range(1, REACH + 1)]
    gradient = adjoint(
        residuals, [own_hours] + hours_of, [prints] + [pair[0] for pair in gathered], samples * hours
    )
    return modeled, gradient.reshape(samples, hours, cells)


def solution(mesh):
    placed = (
        P(None, "tm", "cells"),
        P("tm", None, "cells"),
        P("tm", None),
        P("tm"),
        P("tm", "cells"),
        P(None, "tm"),
        P("tm"),
    )
    return jax.shard_map(
        body,
        mesh=mesh,
        in_specs=placed,
        out_specs=(P(None, "tm"), P(None, "tm", "cells")),
        check_vma=False,
    )
```

```python
import jax
import jax.numpy as jnp
from jax import lax
from jax.experimental import pallas as pl
from jax.experimental.pallas import tpu as pltpu
from jax.sharding import PartitionSpec as P

REACH = 3
TILE = 128
STEP_TILES = 8
WIDTH = STEP_TILES * TILE
ROUND_ROWS = (256, 256, 128)
PIECE = 256
CHUNK_STEPS = (2, 2)
VMEM_BYTES = 48 * 1024 * 1024
WRAP = 4


def shifted(value, steps):
    count = lax.axis_size("tm")
    initial, last = (max(0, -steps), min(count, count - steps))
    return lax.ppermute(value, "tm", [(source, source + steps) for source in range(initial, last)])


def swapped(value):
    return lax.ppermute(value, "cells", [(0, 1), (1, 0)])


def shifted_three(value):
    count = lax.axis_size("tm")
    turned = WRAP - 1
    up = [(source, source - WRAP) for source in range(WRAP, count) if source % WRAP != turned]
    above = lax.ppermute(value, "tm", up)
    there = jnp.where(lax.axis_index("tm") % WRAP == turned, value, above)
    ring = [(source, source - source % WRAP + (source + 1) % WRAP) for source in range(count)]
    return lax.ppermute(there, "tm", ring)


def leave(value, lag):
    return shifted_three(value) if lag == WRAP - 1 else shifted(value, -lag)


def params():
    return pltpu.CompilerParams(vmem_limit_bytes=VMEM_BYTES)


def one_hot(wanted, position):
    return jnp.where(wanted == position, 1.0, 0.0).astype(jnp.bfloat16)


def product(left, right):
    return jnp.dot(left, right, preferred_element_type=jnp.float32)


def pack_body(pieces_ref, place_ref, prints_ref, *refs):
    own_ref, out_refs = refs[-1 - REACH], refs[-REACH:]
    rows = prints_ref.shape[0]
    for tile in range(STEP_TILES):
        cells = slice(tile * TILE, (tile + 1) * TILE)
        for lag, out_ref in enumerate(out_refs):
            place = place_ref[lag + 1, tile : tile + 1, :]
            slots = lax.broadcasted_iota(jnp.int32, (out_ref.shape[0], rows), 0)
            out_ref[:, cells] = product(one_hot(slots, place), prints_ref[:, cells]).astype(jnp.bfloat16)

    def own_piece(piece, carry):
        start = pl.multiple_of(piece * PIECE, PIECE)
        for tile in range(STEP_TILES):
            cells = slice(tile * TILE, (tile + 1) * TILE)
            slots = lax.broadcasted_iota(jnp.int32, (PIECE, rows), 0) + start
            moved = product(one_hot(slots, place_ref[0, tile : tile + 1, :]), prints_ref[:, cells])
            own_ref[pl.ds(start, PIECE), cells] = moved.astype(jnp.bfloat16)
        return carry

    lax.fori_loop(0, pieces_ref[0], own_piece, 0)


def pack(pieces, place, prints, cells, base, own):
    rows, chunk = prints.shape
    inputs = [place, prints]
    in_specs = [
        pl.BlockSpec((REACH + 1, STEP_TILES, rows), lambda step, _: (0, base + step, 0)),
        pl.BlockSpec((rows, WIDTH), lambda step, _: (0, step)),
    ]
    aliases = {}
    if own is not None:
        inputs.append(own)
        in_specs.append(pl.BlockSpec(memory_space=pl.ANY))
        aliases = {3: 0}
    return pl.pallas_call(
        pack_body,
        grid_spec=pltpu.PrefetchScalarGridSpec(
            num_scalar_prefetch=1,
            grid=(chunk // WIDTH,),
            in_specs=in_specs,
            out_specs=[pl.BlockSpec((rows, WIDTH), lambda step, _: (0, base + step))]
            + [pl.BlockSpec((room, WIDTH), lambda step, _: (0, step)) for room in ROUND_ROWS],
        ),
        out_shape=[jax.ShapeDtypeStruct((rows, cells), jnp.bfloat16)]
        + [jax.ShapeDtypeStruct((room, chunk), jnp.bfloat16) for room in ROUND_ROWS],
        input_output_aliases=aliases,
        compiler_params=params(),
        cost_estimate=pl.CostEstimate(
            flops=2 * (sum(ROUND_ROWS) + PIECE) * rows * chunk, bytes_accessed=6 * rows * chunk, transcendentals=0
        ),
        name="pack",
    )(pieces, *inputs)


def add_products(flux_ref, part, sums_ref, at):
    sums_ref[at] += lax.dot_general(
        flux_ref[...], part, (((1,), (1,)), ((), ())), preferred_element_type=jnp.float32
    )


def finish(hour, obs_of, sums, samples):
    samples_hours, piece = sums.shape
    hours = samples_hours // samples
    row_hour = lax.rem(lax.broadcasted_iota(jnp.int32, (samples_hours, piece), 0), hours)
    picked = jnp.sum(jnp.where(hour == row_hour, sums, 0.0).reshape(samples, hours, piece), axis=1)
    to_obs = jnp.where(lax.broadcasted_iota(jnp.int32, (piece, PIECE), 1) == obs_of, 1.0, 0.0)
    return jnp.dot(picked, to_obs, precision=lax.Precision.HIGHEST, preferred_element_type=jnp.float32)


def own_body(pieces_ref, flux_ref, prints_ref, cols_ref, hour_ref, out_ref, sums_ref):
    step = pl.program_id(0)
    tiles = pl.num_programs(0) * STEP_TILES
    del tiles

    @pl.when(step == 0)
    def _():
        sums_ref[...] = jnp.zeros_like(sums_ref)

    def one_piece(piece, carry):
        start = pl.multiple_of(piece * PIECE, PIECE)
        add_products(flux_ref, prints_ref[pl.ds(start, PIECE), :], sums_ref, piece)
        return carry

    lax.fori_loop(0, pieces_ref[0], one_piece, 0)

    @pl.when(step == pl.num_programs(0) - 1)
    def _():
        out_ref[...] = jnp.zeros_like(out_ref)

        def last(piece, carry):
            start = pl.multiple_of(piece * PIECE, PIECE)
            obs_of = cols_ref[0, pl.ds(start, PIECE), :][:, -1:]
            hour = hour_ref[0, pl.ds(piece, 1), :]
            out_ref[...] += finish(hour, obs_of, sums_ref[piece], out_ref.shape[0])
            return carry

        lax.fori_loop(0, pieces_ref[0], last, 0)


def own_products(pieces, flux, prints, cols, hour_of, samples):
    rows, cells = prints.shape
    obs = hour_of.shape[2]
    return pl.pallas_call(
        own_body,
        grid_spec=pltpu.PrefetchScalarGridSpec(
            num_scalar_prefetch=1,
            grid=(cells // WIDTH,),
            in_specs=[
                pl.BlockSpec((flux.shape[0], WIDTH), lambda step, _: (0, step)),
                pl.BlockSpec((rows, WIDTH), lambda step, _: (0, step)),
                pl.BlockSpec((1, rows, TILE), lambda step, _: (0, 0, 0)),
                pl.BlockSpec(hour_of.shape, lambda step, _: (0, 0, 0)),
            ],
            out_specs=pl.BlockSpec((samples, obs), lambda step, _: (0, 0)),
            scratch_shapes=[pltpu.VMEM((rows // PIECE, flux.shape[0], PIECE), jnp.float32)],
        ),
        out_shape=jax.ShapeDtypeStruct((samples, obs), jnp.float32),
        compiler_params=params(),
        cost_estimate=pl.CostEstimate(
            flops=2 * flux.shape[0] * PIECE * cells, bytes_accessed=3 * rows * cells, transcendentals=0
        ),
        name="own_products",
    )(pieces, flux, prints, cols, hour_of)


def unpack_body(base, pieces_ref, flux_ref, *refs):
    moved_refs, (cols_ref, hour_ref) = refs[:REACH], refs[REACH : REACH + 2]
    sums_ref, out_ref, prints_refs = refs[-1], refs[-2], refs[-2 - REACH : -2]
    step = pl.program_id(0)

    @pl.when(step == 0)
    def _():
        sums_ref[...] = jnp.zeros_like(sums_ref)

    turn = lax.rem(TILE - STEP_TILES * (base + step), TILE)
    for lag in range(REACH):
        room = moved_refs[lag].shape[0]

        def one_piece(piece, carry, lag=lag, room=room):
            start = pl.multiple_of(piece * PIECE, PIECE)
            places = pltpu.roll(cols_ref[lag + 1, pl.ds(start, PIECE), :], turn, 1)
            slots = lax.broadcasted_iota(jnp.int32, (PIECE, room), 1)
            for tile in range(STEP_TILES):
                cells = slice(tile * TILE, (tile + 1) * TILE)
                back = product(one_hot(slots, places[:, tile : tile + 1]), moved_refs[lag][:, cells])
                prints_refs[lag][pl.ds(start, PIECE), cells] = back.astype(jnp.bfloat16)
            add_products(flux_ref, prints_refs[lag][pl.ds(start, PIECE), :], sums_ref, (lag, piece))
            return carry

        lax.fori_loop(0, pieces_ref[lag + 1], one_piece, 0)

    @pl.when(step == pl.num_programs(0) - 1)
    def _():
        out_ref[...] = jnp.zeros_like(out_ref)
        for lag in range(REACH):

            def last(piece, carry, lag=lag):
                start = pl.multiple_of(piece * PIECE, PIECE)
                obs_of = cols_ref[lag + 1, pl.ds(start, PIECE), :][:, -1:]
                hour = hour_ref[lag + 1, pl.ds(piece, 1), :]
                out_ref[lag] += finish(hour, obs_of, sums_ref[lag, piece], out_ref.shape[1])
                return carry

            lax.fori_loop(0, pieces_ref[lag + 1], last, 0)


def unpack_products(pieces, flux, moved, cols, hour_of, samples, base, prints):
    rows = cols.shape[1]
    obs = hour_of.shape[2]
    cells = flux.shape[1]
    chunk = moved[0].shape[1]
    inputs = [flux, *moved, cols, hour_of]
    in_specs = (
        [pl.BlockSpec((flux.shape[0], WIDTH), lambda step, _: (0, base + step))]
        + [pl.BlockSpec((part.shape[0], WIDTH), lambda step, _: (0, step)) for part in moved]
        + [
            pl.BlockSpec(cols.shape, lambda step, _: (0, 0, 0)),
            pl.BlockSpec(hour_of.shape, lambda step, _: (0, 0, 0)),
        ]
    )
    aliases = {}
    if prints is not None:
        aliases = {1 + len(inputs) + lag: lag for lag in range(REACH)}
        inputs += prints
        in_specs += [pl.BlockSpec(memory_space=pl.ANY)] * REACH

    def kernel(*refs):
        unpack_body(base, *refs)

    return pl.pallas_call(
        kernel,
        grid_spec=pltpu.PrefetchScalarGridSpec(
            num_scalar_prefetch=1,
            grid=(chunk // WIDTH,),
            in_specs=in_specs,
            out_specs=[pl.BlockSpec((rows, WIDTH), lambda step, _: (0, base + step))] * REACH
            + [pl.BlockSpec((REACH, samples, obs), lambda step, _: (0, 0, 0))],
            scratch_shapes=[pltpu.VMEM((REACH, rows // PIECE, flux.shape[0], PIECE), jnp.float32)],
        ),
        out_shape=[jax.ShapeDtypeStruct((rows, cells), jnp.bfloat16)] * REACH
        + [jax.ShapeDtypeStruct((REACH, samples, obs), jnp.float32)],
        input_output_aliases=aliases,
        compiler_params=params(),
        cost_estimate=pl.CostEstimate(
            flops=10 * (flux.shape[0] + PIECE) * PIECE * chunk, bytes_accessed=8 * rows * chunk, transcendentals=0
        ),
        name="unpack_products",
    )(pieces, *inputs)


def adjoint_body(pieces_ref, *refs):
    count = REACH + 1
    residual_refs, (hour_ref, obs_ref), prints_refs = refs[:count], refs[count : count + 2], refs[count + 2 : -2]
    out_ref, spread_ref = refs[-2:]
    samples_hours, piece_rows = spread_ref.shape[2:]
    samples, obs = residual_refs[0].shape
    hours = samples_hours // samples

    @pl.when(pl.program_id(0) == 0)
    def _():
        row_hour = lax.broadcasted_iota(jnp.int32, (samples, hours, piece_rows), 1)
        for lag in range(count):

            def spread_piece(piece, carry, lag=lag):
                slots = lax.broadcasted_iota(jnp.int32, (obs, piece_rows), 0)
                value = product(residual_refs[lag][...], one_hot(slots, obs_ref[lag, pl.ds(piece, 1), :]))
                value = jnp.broadcast_to(value[:, None, :], (samples, hours, piece_rows))
                wanted = hour_ref[lag, pl.ds(piece, 1), :][None]
                spread = jnp.where(wanted == row_hour, value, 0.0).reshape(samples_hours, piece_rows)
                spread_ref[lag, piece] = spread.astype(jnp.bfloat16)
                return carry

            lax.fori_loop(0, pieces_ref[lag], spread_piece, 0)

    out_ref[...] = jnp.zeros_like(out_ref)
    for lag in range(count):

        def one_piece(piece, carry, lag=lag):
            start = pl.multiple_of(piece * PIECE, PIECE)
            out_ref[...] += product(spread_ref[lag, piece], prints_refs[lag][pl.ds(start, PIECE), :])
            return carry

        lax.fori_loop(0, pieces_ref[lag], one_piece, 0)


def adjoint(pieces, residuals, hour_of, obs_of, prints, samples_hours, width=512):
    rows, cells = prints[0].shape
    count = REACH + 1
    return pl.pallas_call(
        adjoint_body,
        grid_spec=pltpu.PrefetchScalarGridSpec(
            num_scalar_prefetch=1,
            grid=(cells // width,),
            in_specs=[pl.BlockSpec(residuals[0].shape, lambda step, _: (0, 0))] * count
            + [pl.BlockSpec(hour_of.shape, lambda step, _: (0, 0, 0))] * 2
            + [pl.BlockSpec((rows, width), lambda step, _: (0, step))] * count,
            out_specs=pl.BlockSpec((samples_hours, width), lambda step, _: (0, step)),
            scratch_shapes=[pltpu.VMEM((count, rows // PIECE, samples_hours, PIECE), jnp.bfloat16)],
        ),
        out_shape=jax.ShapeDtypeStruct((samples_hours, cells), jnp.float32),
        compiler_params=params(),
        cost_estimate=pl.CostEstimate(
            flops=12 * samples_hours * PIECE * cells, bytes_accessed=10 * rows * cells, transcendentals=0
        ),
        name="adjoint",
    )(pieces, *residuals, hour_of, obs_of, *prints)


def body(flux, footprint, band_lag, obs_hour, tile_mask, obs_value, obs_weight):
    samples, hours, cells = flux.shape
    obs, bands, _ = footprint.shape
    tiles = tile_mask.shape[1]
    rows = bands * obs
    position = lax.axis_index("tm")
    flux_rows = flux.reshape(samples * hours, cells)

    source = (obs_hour[:, None] - band_lag).T
    mask = tile_mask.T
    note = jnp.concatenate([mask, source, jnp.zeros((8 - bands, obs), jnp.int32)], axis=0)
    notes = [note] + [shifted(note, -lag) for lag in range(1, REACH + 1)]

    def hour_in(hour, block):
        inside = hour - block * hours
        return jnp.where((inside >= 0) & (inside < hours), inside, -1).reshape(rows)

    down = lax.broadcasted_iota(jnp.int32, (rows, rows), 0)
    along = lax.broadcasted_iota(jnp.int32, (rows, rows), 1)
    before = (down < along).astype(jnp.bfloat16)

    to_block = jnp.stack([hour_in(source, position - lag) >= 0 for lag in range(REACH + 1)])
    on = jnp.tile(mask, (1, bands)) > 0
    leaving = to_block[:, None, :] & on[None]
    ranked = jnp.concatenate([jnp.broadcast_to(to_block[:1, None, :], (1, tiles, rows)), leaving[1:]], axis=0)
    place = lax.dot_general(
        ranked.astype(jnp.bfloat16), before, (((2,), (0,)), ((), ())), preferred_element_type=jnp.float32
    )
    place = jnp.where(leaving, place.astype(jnp.int32), -1)
    own_pieces = (jnp.sum(to_block[:1].astype(jnp.int32), axis=1) + PIECE - 1) // PIECE
    counts = jnp.max(jnp.sum(leaving[1:].astype(jnp.int32), axis=2), axis=1)
    room = jnp.array(ROUND_ROWS, jnp.int32)
    need = jnp.max((counts + room - 1) // room)

    starts = [sum(CHUNK_STEPS[:chunk]) for chunk in range(len(CHUNK_STEPS))]

    def prints_of(chunk):
        first, last = starts[chunk] * WIDTH, (starts[chunk] + CHUNK_STEPS[chunk]) * WIDTH
        return footprint[:, :, first:last].transpose(1, 0, 2).reshape(rows, last - first)

    chunks = range(len(CHUNK_STEPS))
    prints, moved, own = [], [], None
    for chunk in chunks:
        prints.append(prints_of(chunk))
        own, *packed = pack(own_pieces, place, prints[chunk], cells, starts[chunk], own)
        moved.append([leave(part, lag + 1) for lag, part in enumerate(packed)])

    need, own = lax.optimization_barrier((need, own))
    everyone = lax.axis_size("tm") * lax.axis_size("cells")
    needs = jnp.broadcast_to(need, (everyone, TILE))
    rounds = jnp.max(lax.all_to_all(needs, ("tm", "cells"), 0, 0, tiled=True))

    their_mask = jnp.stack([part[:tiles] for part in notes])
    their_hour = jnp.stack([hour_in(part[tiles : tiles + bands], position) for part in notes])
    coming = their_hour >= 0
    rank = jnp.dot(coming.astype(jnp.bfloat16), before, preferred_element_type=jnp.float32)
    rank = jnp.where(coming, rank.astype(jnp.int32), -1)
    pieces = (jnp.sum(coming.astype(jnp.int32), axis=1) + PIECE - 1) // PIECE
    facts = jnp.concatenate(
        [
            jnp.tile(their_mask, (1, 1, bands)),
            their_hour[:, None, :],
            jnp.broadcast_to(jnp.tile(jnp.arange(obs, dtype=jnp.int32), bands)[None, None], (REACH + 1, 1, rows)),
        ],
        axis=1,
    ).astype(jnp.bfloat16)
    sorter = (rank[:, None, :] == down[None]).astype(jnp.bfloat16)
    facts = lax.dot_general(sorter, facts, (((2,), (2,)), ((0,), (0,))), preferred_element_type=jnp.float32)
    there = facts[:, :, :tiles]
    spot = lax.dot_general(
        before, there.astype(jnp.bfloat16), (((0,), (1,)), ((), ())), preferred_element_type=jnp.float32
    ).transpose(1, 0, 2)
    facts = facts.astype(jnp.int32)
    spot = jnp.where(there > 0, spot.astype(jnp.int32), -1)
    cols = jnp.concatenate(
        [spot, jnp.zeros((REACH + 1, rows, TILE - tiles - 1), jnp.int32), facts[:, :, tiles + 1 :]], axis=2
    )
    hour_of = facts[:, :, tiles].reshape(REACH + 1, rows // PIECE, PIECE)
    obs_of = facts[:, :, tiles + 1].reshape(REACH + 1, rows // PIECE, PIECE)

    own_partial = own_products(pieces, flux_rows, own, cols, hour_of, samples)
    moved, own_partial = lax.optimization_barrier((moved, own_partial))

    def unpack_all(arrived, cols):
        total, restored = 0.0, None
        for chunk in chunks:
            *restored, part = unpack_products(
                pieces, flux_rows, arrived[chunk], cols, hour_of, samples, starts[chunk], restored
            )
            total = total + part
        return restored, total

    state = unpack_all(moved, cols)

    def further(index, state):
        lower = index * jnp.concatenate([jnp.zeros((1,), jnp.int32), room])
        unused, arrived = None, []
        for chunk in chunks:
            unused, *packed = pack(
                own_pieces, place - lower[:, None, None], prints[chunk], cells, starts[chunk], unused
            )
            arrived.append([shifted(part, -lag - 1) for lag, part in enumerate(packed)])
        lane = lax.broadcasted_iota(jnp.int32, cols.shape, 2)
        more, added = unpack_all(arrived, jnp.where(lane < tiles, cols - lower[:, None, None], cols))
        restored, total = state
        return [a + b for a, b in zip(restored, more)], total + added

    restored, total = lax.fori_loop(1, rounds, further, state)

    partial = own_partial
    for lag in range(REACH):
        partial = partial + shifted(total[lag], lag + 1)
    modeled = partial + swapped(partial)
    residual = (obs_weight[None, :] * (modeled - obs_value)).astype(jnp.bfloat16)
    residuals = [residual] + [shifted(residual, -lag) for lag in range(1, REACH + 1)]
    gradient = adjoint(pieces, residuals, hour_of, obs_of, [own, *restored], samples * hours)
    return modeled, gradient.reshape(samples, hours, cells)


def solution(mesh):
    placed = (
        P(None, "tm", "cells"),
        P("tm", None, "cells"),
        P("tm", None),
        P("tm"),
        P("tm", "cells"),
        P(None, "tm"),
        P("tm"),
    )
    return jax.shard_map(
        body,
        mesh=mesh,
        in_specs=placed,
        out_specs=(P(None, "tm"), P(None, "tm", "cells")),
        check_vma=False,
    )
```

```python
import jax
import jax.numpy as jnp
from jax import lax
from jax.experimental import pallas as pl
from jax.experimental.pallas import tpu as pltpu
from jax.sharding import PartitionSpec as P

REACH = 3
TILE = 128
STEP_TILES = 8
WIDTH = STEP_TILES * TILE
ROUND_ROWS = (256, 256, 128)
PIECE_ROWS = (256, 512, 512, 256)
SMALL = pl.CostEstimate(flops=1000, bytes_accessed=1000, transcendentals=0)
CHUNK_STEPS = (2, 2)
VMEM_BYTES = 48 * 1024 * 1024
WRAP = 4


def shifted(value, steps):
    count = lax.axis_size("tm")
    initial, last = (max(0, -steps), min(count, count - steps))
    return lax.ppermute(value, "tm", [(source, source + steps) for source in range(initial, last)])


def swapped(value):
    return lax.ppermute(value, "cells", [(0, 1), (1, 0)])


def shifted_three(value):
    count = lax.axis_size("tm")
    turned = WRAP - 1
    up = [(source, source - WRAP) for source in range(WRAP, count) if source % WRAP != turned]
    above = lax.ppermute(value, "tm", up)
    there = jnp.where(lax.axis_index("tm") % WRAP == turned, value, above)
    ring = [(source, source - source % WRAP + (source + 1) % WRAP) for source in range(count)]
    return lax.ppermute(there, "tm", ring), above


def params():
    return pltpu.CompilerParams(vmem_limit_bytes=VMEM_BYTES)


def one_hot(wanted, position):
    return jnp.where(wanted == position, 1.0, 0.0).astype(jnp.bfloat16)


def product(left, right):
    return jnp.dot(left, right, preferred_element_type=jnp.float32)


def pack_body(place_ref, prints_ref, *out_refs):
    rows = prints_ref.shape[0]
    for tile in range(STEP_TILES):
        cells = slice(tile * TILE, (tile + 1) * TILE)
        for lag, out_ref in enumerate(out_refs):
            place = place_ref[lag + 1, tile : tile + 1, :]
            slots = lax.broadcasted_iota(jnp.int32, (out_ref.shape[0], rows), 0)
            out_ref[:, cells] = product(one_hot(slots, place), prints_ref[:, cells]).astype(jnp.bfloat16)


def pack(place, prints, base):
    rows, chunk = prints.shape
    return pl.pallas_call(
        pack_body,
        grid=(chunk // WIDTH,),
        in_specs=[
            pl.BlockSpec((REACH + 1, STEP_TILES, rows), lambda step: (0, base + step, 0)),
            pl.BlockSpec((rows, WIDTH), lambda step: (0, step)),
        ],
        out_specs=[pl.BlockSpec((room, WIDTH), lambda step: (0, step)) for room in ROUND_ROWS],
        out_shape=[jax.ShapeDtypeStruct((room, chunk), jnp.bfloat16) for room in ROUND_ROWS],
        compiler_params=params(),
        cost_estimate=SMALL,
        name="pack",
    )(place, prints)


def pieces_in(lag, rows):
    size = PIECE_ROWS[lag]
    return [(piece, slice(piece * size, (piece + 1) * size)) for piece in range(rows // size)]


def multiply(flux_ref, part, sums_ref, piece):
    sums_ref[piece] += lax.dot_general(
        flux_ref[...], part, (((1,), (1,)), ((), ())), preferred_element_type=jnp.float32
    )


def finish(hour, obs_of, sums, samples, obs):
    samples_hours, size = sums.shape
    hours = samples_hours // samples
    row_hour = lax.rem(lax.broadcasted_iota(jnp.int32, (samples_hours, size), 0), hours)
    picked = jnp.sum(jnp.where(hour == row_hour, sums, 0.0).reshape(samples, hours, size), axis=1)
    to_obs = jnp.where(lax.broadcasted_iota(jnp.int32, (size, obs), 1) == obs_of, 1.0, 0.0)
    return jnp.dot(picked, to_obs, precision=lax.Precision.HIGHEST, preferred_element_type=jnp.float32)


def restore_body(lags, base, counts_ref, flux_ref, *refs):
    source_refs = refs[: len(lags)]
    place_ref, cols_ref, facts_ref = refs[len(lags) : len(lags) + 3]
    scratch = refs[-len(lags) :]
    out_ref = refs[-len(lags) - 1]
    rows = cols_ref.shape[1]
    total = sum(len(pieces_in(lag, rows)) for lag in lags)
    kept_refs = list(refs[-len(lags) - 1 - total : -len(lags) - 1])
    step = pl.program_id(0)
    final = step == pl.num_programs(0) - 1
    samples, obs = out_ref.shape[1:]

    @pl.when(step == 0)
    def _():
        out_ref[...] = jnp.zeros_like(out_ref)

    turn = lax.rem(TILE - STEP_TILES * (base + step), TILE)
    for index, lag in enumerate(lags):
        source_ref, sums_ref = source_refs[index], scratch[index]
        room = source_ref.shape[0]
        for piece, span in pieces_in(lag, rows):
            kept_ref = kept_refs.pop(0)
            size = kept_ref.shape[0]

            @pl.when(piece < counts_ref[lag])
            def _(lag=lag, index=index, piece=piece, span=span, kept_ref=kept_ref, size=size, room=room,
                  source_ref=source_ref, sums_ref=sums_ref):
                if lag == 0:
                    slots = lax.broadcasted_iota(jnp.int32, (size, room), 0) + span.start
                else:
                    places = pltpu.roll(cols_ref[index, span, :], turn, 1)
                    slots = lax.broadcasted_iota(jnp.int32, (size, room), 1)
                for tile in range(STEP_TILES):
                    cells = slice(tile * TILE, (tile + 1) * TILE)
                    place = place_ref[0, tile : tile + 1, :] if lag == 0 else places[:, tile : tile + 1]
                    back = product(one_hot(slots, place), source_ref[:, cells])
                    kept_ref[:, cells] = back.astype(jnp.bfloat16)

                @pl.when(step == 0)
                def _():
                    sums_ref[piece] = jnp.zeros(sums_ref.shape[1:], jnp.float32)

                multiply(flux_ref, kept_ref[...], sums_ref, piece)

                @pl.when(final)
                def _():
                    hour, obs_of = facts_ref[index, 6:7, span], cols_ref[index, span, :][:, -1:]
                    out_ref[index] += finish(hour, obs_of, sums_ref[piece], samples, obs)


def restore(lags, counts, flux, sources, place, cols, facts, samples, obs, base, kept):
    rows = cols.shape[1]
    cells, chunk = flux.shape[1], sources[0].shape[1]
    inputs = [flux, *sources, place, cols, facts]
    in_specs = (
        [pl.BlockSpec((flux.shape[0], WIDTH), lambda step, _: (0, base + step))]
        + [pl.BlockSpec((part.shape[0], WIDTH), lambda step, _: (0, step)) for part in sources]
        + [
            pl.BlockSpec((1, STEP_TILES, rows), lambda step, _: (0, base + step, 0)),
            pl.BlockSpec(cols.shape, lambda step, _: (0, 0, 0)),
            pl.BlockSpec(facts.shape, lambda step, _: (0, 0, 0)),
        ]
    )
    pieces = [(lag, piece) for lag in lags for piece, _ in pieces_in(lag, rows)]
    aliases = {}
    if kept is not None:
        aliases = {1 + len(inputs) + index: index for index in range(len(pieces))}
        inputs += kept
        in_specs += [pl.BlockSpec(memory_space=pl.ANY)] * len(pieces)

    def kept_spec(lag, piece):
        return pl.BlockSpec(
            (PIECE_ROWS[lag], WIDTH), lambda step, counts: (0, jnp.where(piece < counts[lag], base + step, base))
        )

    def kernel(*refs):
        restore_body(lags, base, *refs)

    *kept, partial = pl.pallas_call(
        kernel,
        grid_spec=pltpu.PrefetchScalarGridSpec(
            num_scalar_prefetch=1,
            grid=(chunk // WIDTH,),
            in_specs=in_specs,
            out_specs=[kept_spec(lag, piece) for lag, piece in pieces]
            + [pl.BlockSpec((len(lags), samples, obs), lambda step, _: (0, 0, 0))],
            scratch_shapes=[
                pltpu.VMEM((rows // PIECE_ROWS[lag], flux.shape[0], PIECE_ROWS[lag]), jnp.float32) for lag in lags
            ],
        ),
        out_shape=[jax.ShapeDtypeStruct((PIECE_ROWS[lag], cells), jnp.bfloat16) for lag, _ in pieces]
        + [jax.ShapeDtypeStruct((len(lags), samples, obs), jnp.float32)],
        input_output_aliases=aliases,
        compiler_params=params(),
        cost_estimate=SMALL,
        name="restore",
    )(counts, *inputs)
    return kept, partial


def describe_body(blocks_ref, first_ref, note_ref, cols_ref, facts_ref):
    tiles = note_ref.shape[1] - 8
    obs, rows = note_ref.shape[2], cols_ref.shape[1]
    bands = rows // obs
    hours = first_ref[1]
    inside = jnp.concatenate([note_ref[0, tiles + band : tiles + band + 1, :] for band in range(bands)], axis=1)
    inside = inside - first_ref[0]
    coming = (inside >= 0) & (inside < hours)
    ones = jnp.where(coming, 1.0, 0.0)
    split = jnp.concatenate([ones[:, at : at + TILE] for at in range(0, rows, TILE)], axis=0)
    down = lax.broadcasted_iota(jnp.int32, (TILE, TILE), 0)
    ahead = jnp.where(down < lax.broadcasted_iota(jnp.int32, (TILE, TILE), 1), 1.0, 0.0).astype(jnp.bfloat16)
    within = product(split.astype(jnp.bfloat16), ahead)
    totals = jnp.sum(split, axis=1, keepdims=True)
    ranks, carried = [], jnp.zeros((1, 1), jnp.float32)
    for index in range(rows // TILE):
        ranks.append(within[index : index + 1, :] + carried)
        carried = carried + totals[index : index + 1, :]
    rank = jnp.where(coming, jnp.concatenate(ranks, axis=1), -1.0).astype(jnp.int32)
    hour = jnp.where(coming, inside, 0).astype(jnp.float32)
    obs_of = lax.rem(lax.broadcasted_iota(jnp.int32, (1, rows), 1), obs).astype(jnp.float32)
    on = note_ref[0, :tiles, :].astype(jnp.float32)
    table = jnp.concatenate(
        [jnp.concatenate([on] * bands, axis=1), jnp.zeros((TILE - tiles - 2, rows), jnp.float32), hour, obs_of], axis=0
    ).astype(jnp.bfloat16)
    size = PIECE_ROWS[0]
    below = lax.broadcasted_iota(jnp.int32, (size, size), 1) < lax.broadcasted_iota(jnp.int32, (size, size), 0)
    below = jnp.where(below, 1.0, 0.0).astype(jnp.bfloat16)
    lane = lax.broadcasted_iota(jnp.int32, (size, TILE), 1)
    both = (((1,), (1,)), ((), ()))
    sofar = jnp.zeros((1, TILE), jnp.float32)
    for piece in range(rows // size):
        span = slice(piece * size, (piece + 1) * size)
        sorter = one_hot(lax.broadcasted_iota(jnp.int32, (size, rows), 0) + span.start, rank)
        found = lax.dot_general(sorter, table, both, preferred_element_type=jnp.float32)
        place = product(below, found.astype(jnp.bfloat16)) + sofar
        sofar = sofar + jnp.sum(found, axis=0, keepdims=True)
        cols_ref[0, span, :] = jnp.where(lane < tiles, jnp.where(found > 0.0, place, -1.0), found).astype(jnp.int32)
        flat = lax.dot_general(table[TILE - 16 :], sorter, both, preferred_element_type=jnp.float32)
        facts_ref[0, :, span] = flat[8:].astype(jnp.int32)


def describe(first, notes, rows):
    count, height, obs = notes.shape
    return pl.pallas_call(
        describe_body,
        grid_spec=pltpu.PrefetchScalarGridSpec(
            num_scalar_prefetch=2,
            grid=(count,),
            in_specs=[pl.BlockSpec((1, height, obs), lambda step, *_: (step, 0, 0))],
            out_specs=[
                pl.BlockSpec((1, rows, TILE), lambda step, *_: (step, 0, 0)),
                pl.BlockSpec((1, 8, rows), lambda step, *_: (step, 0, 0)),
            ],
        ),
        out_shape=[
            jax.ShapeDtypeStruct((count, rows, TILE), jnp.int32),
            jax.ShapeDtypeStruct((count, 8, rows), jnp.int32),
        ],
        compiler_params=params(),
        cost_estimate=SMALL,
        name="describe",
    )(first, first, notes)


def adjoint_body(counts_ref, *refs):
    count = REACH + 1
    residual_refs, own_facts_ref, facts_ref = refs[:count], refs[count], refs[count + 1]
    spread_refs, out_ref = refs[-count:], refs[-count - 1]
    kept_refs = refs[count + 2 : -count - 1]
    rows = facts_ref.shape[2]
    samples, obs = residual_refs[0].shape
    samples_hours = out_ref.shape[0]
    hours = samples_hours // samples
    pieces = [(lag, piece, span) for lag in range(count) for piece, span in pieces_in(lag, rows)]

    @pl.when(pl.program_id(0) == 0)
    def _():
        for lag, piece, span in pieces:

            @pl.when(piece < counts_ref[lag])
            def _(lag=lag, piece=piece, span=span):
                size = span.stop - span.start
                slots = lax.broadcasted_iota(jnp.int32, (obs, size), 0)
                its_hour = own_facts_ref[0, 6:7, span] if lag == 0 else facts_ref[lag - 1, 6:7, span]
                its_obs = own_facts_ref[0, 7:8, span] if lag == 0 else facts_ref[lag - 1, 7:8, span]
                value = product(residual_refs[lag][...], one_hot(slots, its_obs))
                value = jnp.broadcast_to(value[:, None, :], (samples, hours, size))
                row_hour = lax.broadcasted_iota(jnp.int32, (samples, hours, size), 1)
                spread = jnp.where(its_hour[None] == row_hour, value, 0.0).reshape(samples_hours, size)
                spread_refs[lag][piece] = spread.astype(jnp.bfloat16)

    total = None
    for index, (lag, piece, _) in enumerate(pieces):
        if piece == 0:
            term = product(spread_refs[lag][0], kept_refs[index][...])
            total = term if total is None else total + term
    out_ref[...] = total
    for index, (lag, piece, _) in enumerate(pieces):
        if piece > 0:

            @pl.when(piece < counts_ref[lag])
            def _(index=index, lag=lag, piece=piece):
                out_ref[...] += product(spread_refs[lag][piece], kept_refs[index][...])


def adjoint(counts, residuals, own_facts, facts, kept, samples_hours, width=512):
    rows, cells = facts.shape[2], kept[0].shape[1]
    count = REACH + 1
    pieces = [(lag, piece) for lag in range(count) for piece, _ in pieces_in(lag, rows)]

    def kept_spec(lag, piece):
        return pl.BlockSpec(
            (PIECE_ROWS[lag], width), lambda step, counts: (0, jnp.where(piece < counts[lag], step, 0))
        )

    return pl.pallas_call(
        adjoint_body,
        grid_spec=pltpu.PrefetchScalarGridSpec(
            num_scalar_prefetch=1,
            grid=(cells // width,),
            in_specs=[pl.BlockSpec(residuals[0].shape, lambda step, _: (0, 0))] * count
            + [pl.BlockSpec(part.shape, lambda step, _: (0, 0, 0)) for part in (own_facts, facts)]
            + [kept_spec(lag, piece) for lag, piece in pieces],
            out_specs=pl.BlockSpec((samples_hours, width), lambda step, _: (0, step)),
            scratch_shapes=[
                pltpu.VMEM((rows // size, samples_hours, size), jnp.bfloat16) for size in PIECE_ROWS
            ],
        ),
        out_shape=jax.ShapeDtypeStruct((samples_hours, cells), jnp.float32),
        compiler_params=params(),
        cost_estimate=SMALL,
        name="adjoint",
    )(counts, *residuals, own_facts, facts, *kept)


def body(flux, footprint, band_lag, obs_hour, tile_mask, obs_value, obs_weight):
    samples, hours, cells = flux.shape
    obs, bands, _ = footprint.shape
    tiles = tile_mask.shape[1]
    rows = bands * obs
    position = lax.axis_index("tm")
    flux_rows = flux.reshape(samples * hours, cells)

    source = (obs_hour[:, None] - band_lag).T
    mask = tile_mask.T
    note = jnp.concatenate([mask, source, jnp.zeros((8 - bands, obs), jnp.int32)], axis=0)

    def hour_in(hour, block):
        inside = hour - block * hours
        return jnp.where((inside >= 0) & (inside < hours), inside, -1).reshape(rows)

    down = lax.broadcasted_iota(jnp.int32, (rows, rows), 0)
    along = lax.broadcasted_iota(jnp.int32, (rows, rows), 1)
    before = (down < along).astype(jnp.bfloat16)

    to_block = jnp.stack([hour_in(source, position - lag) >= 0 for lag in range(REACH + 1)])
    on = jnp.tile(mask, (1, bands)) > 0
    leaving = to_block[:, None, :] & on[None]
    ranked = jnp.concatenate([jnp.broadcast_to(to_block[:1, None, :], (1, tiles, rows)), leaving[1:]], axis=0)
    place = lax.dot_general(
        ranked.astype(jnp.bfloat16), before, (((2,), (0,)), ((), ())), preferred_element_type=jnp.float32
    )
    place = jnp.where(leaving, place.astype(jnp.int32), -1)
    counts = jnp.max(jnp.sum(leaving[1:].astype(jnp.int32), axis=2), axis=1)
    room = jnp.array(ROUND_ROWS, jnp.int32)
    need = jnp.max((counts + room - 1) // room)

    starts = [sum(CHUNK_STEPS[:chunk]) for chunk in range(len(CHUNK_STEPS))]

    def prints_of(chunk, footprint):
        first, last = starts[chunk] * WIDTH, (starts[chunk] + CHUNK_STEPS[chunk]) * WIDTH
        return footprint[:, :, first:last].transpose(1, 0, 2).reshape(rows, last - first)

    chunks = range(len(CHUNK_STEPS))
    prints, packs, moved = [], [], []
    for chunk in chunks:
        if packs:
            footprint, packs[-1] = lax.optimization_barrier((footprint, packs[-1]))
        prints.append(prints_of(chunk, footprint))
        packs.append(pack(place, prints[chunk], starts[chunk]))
    sent, packs[0] = lax.optimization_barrier((note, packs[0]))
    notes = [shifted(sent, -lag) for lag in range(1, REACH + 1)]
    for chunk in chunks:
        moved.append([shifted(part, -lag - 1) for lag, part in enumerate(packs[chunk][:-1])])
        third, passing = shifted_three(packs[chunk][-1])
        moved[chunk].append(third)

    first = jnp.stack([position * hours, jnp.int32(hours)])
    def counts_of(parts):
        hour = jnp.stack([hour_in(part[tiles : tiles + bands], position) for part in parts])
        sizes = jnp.array(PIECE_ROWS[: len(parts)], jnp.int32)
        return jnp.maximum((jnp.sum((hour >= 0).astype(jnp.int32), axis=1) + sizes - 1) // sizes, 1)

    own_note, _ = lax.optimization_barrier((note, passing))
    own_count = counts_of([own_note])
    own_cols, own_facts = describe(first, own_note[None], rows)

    own, own_partial = None, 0.0
    for chunk in chunks:
        own, part = restore(
            (0,), own_count, flux_rows, [prints[chunk]], place, own_cols, own_facts, samples, obs, starts[chunk], own
        )
        own_partial = own_partial + part[0]
    *moved[0], own_partial, notes, need = lax.optimization_barrier((*moved[0], own_partial, notes, need))
    everyone = lax.axis_size("tm") * lax.axis_size("cells")
    needs = jnp.broadcast_to(need, (everyone, TILE))
    rounds = jnp.max(lax.all_to_all(needs, ("tm", "cells"), 0, 0, tiled=True))

    cols, facts = describe(first, jnp.stack(notes), rows)
    counts = counts_of([note] + list(notes))

    def restore_all(arrived, cols):
        total, kept = 0.0, None
        for chunk in chunks:
            kept, part = restore(
                tuple(range(1, REACH + 1)), counts, flux_rows, arrived[chunk], place, cols, facts, samples, obs,
                starts[chunk], kept,
            )
            total = total + part
        return kept, total

    state = restore_all(moved, cols)

    def further(index, state):
        lower = index * jnp.concatenate([jnp.zeros((1,), jnp.int32), room])
        arrived = []
        for chunk in chunks:
            packed = pack(place - lower[:, None, None], prints[chunk], starts[chunk])
            arrived.append([shifted(part, -lag - 1) for lag, part in enumerate(packed)])
        lane = lax.broadcasted_iota(jnp.int32, cols.shape, 2)
        more, added = restore_all(arrived, jnp.where(lane < tiles, cols - lower[1:, None, None], cols))
        kept, total = state
        return [a + b for a, b in zip(kept, more)], total + added

    kept, total = lax.fori_loop(1, rounds, further, state)

    column = position % WRAP
    cores = lax.axis_size("cells")
    by_lag = jnp.concatenate([own_partial[None], total] * 2)
    slots = lax.dynamic_slice_in_dim(by_lag, (WRAP - column) % WRAP, WRAP)
    group = WRAP * cores
    rows_of_chips = [list(range(at, at + group)) for at in range(0, everyone, group)]
    sums = lax.all_to_all(
        jnp.repeat(slots, cores, axis=0), ("tm", "cells"), 0, 0, axis_index_groups=rows_of_chips, tiled=True
    )
    sums = jnp.sum(sums.reshape(WRAP, cores, samples, obs), axis=1)
    here = (jnp.arange(WRAP) <= column)[:, None, None]
    across = jnp.sum(jnp.where(here, 0.0, sums), axis=0)
    modeled = jnp.sum(jnp.where(here, sums, 0.0), axis=0) + shifted(across, WRAP)
    residual = (obs_weight[None, :] * (modeled - obs_value)).astype(jnp.bfloat16)
    above = shifted(residual, -WRAP)
    slots = jnp.where(here, residual[None], above[None])
    lines = [list(range(at, at + WRAP)) for at in range(0, lax.axis_size("tm"), WRAP)]
    shared = lax.all_to_all(slots, "tm", 0, 0, axis_index_groups=lines, tiled=True)
    shared = lax.dynamic_slice_in_dim(jnp.concatenate([shared] * 2), column, WRAP)
    residuals = [shared[lag] for lag in range(REACH + 1)]
    gradient = adjoint(counts, residuals, own_facts, facts, own + list(kept), samples * hours)
    return modeled, gradient.reshape(samples, hours, cells)


def solution(mesh):
    placed = (
        P(None, "tm", "cells"),
        P("tm", None, "cells"),
        P("tm", None),
        P("tm"),
        P("tm", "cells"),
        P(None, "tm"),
        P("tm"),
    )
    return jax.shard_map(
        body,
        mesh=mesh,
        in_specs=placed,
        out_specs=(P(None, "tm"), P(None, "tm", "cells")),
        check_vma=False,
    )
```

```python
import jax
import jax.numpy as jnp
from jax import lax
from jax.experimental import pallas as pl
from jax.experimental.pallas import tpu as pltpu
from jax.sharding import PartitionSpec as P

REACH = 3
TILE = 128
STEP_TILES = 8
WIDTH = STEP_TILES * TILE
ROUND_ROWS = (256, 256, 128)
NOTE_ROWS = 16
PIECE_ROWS = (256, 512, 512, 256)
SMALL = pl.CostEstimate(flops=1000, bytes_accessed=1000, transcendentals=0)
CHUNK_STEPS = (3, 1)
VMEM_BYTES = 48 * 1024 * 1024
WRAP = 4


def shifted(value, steps):
    count = lax.axis_size("tm")
    initial, last = (max(0, -steps), min(count, count - steps))
    return lax.ppermute(value, "tm", [(source, source + steps) for source in range(initial, last)])


def swapped(value):
    return lax.ppermute(value, "cells", [(0, 1), (1, 0)])


def shifted_three(value):
    count = lax.axis_size("tm")
    turned = WRAP - 1
    up = [(source, source - WRAP) for source in range(WRAP, count) if source % WRAP != turned]
    above = lax.ppermute(value, "tm", up)
    there = jnp.where(lax.axis_index("tm") % WRAP == turned, value, above)
    ring = [(source, source - source % WRAP + (source + 1) % WRAP) for source in range(count)]
    return lax.ppermute(there, "tm", ring), above


def params():
    return pltpu.CompilerParams(vmem_limit_bytes=VMEM_BYTES)


def one_hot(wanted, position):
    return jnp.where(wanted == position, 1.0, 0.0).astype(jnp.bfloat16)


def product(left, right):
    return jnp.dot(left, right, preferred_element_type=jnp.float32)


def pack_body(place_ref, prints_ref, *refs):
    rows = prints_ref.shape[0]
    out_refs = refs[-REACH:]
    for room, out_ref in zip(ROUND_ROWS, out_refs):
        if len(refs) > REACH:
            out_ref[room:, :] = refs[0][...]
    for tile in range(STEP_TILES):
        cells = slice(tile * TILE, (tile + 1) * TILE)
        for lag, out_ref in enumerate(out_refs):
            place = place_ref[lag + 1, tile : tile + 1, :]
            room = ROUND_ROWS[lag]
            slots = lax.broadcasted_iota(jnp.int32, (room, rows), 0)
            out_ref[:room, cells] = product(one_hot(slots, place), prints_ref[:, cells]).astype(jnp.bfloat16)


def pack(place, prints, base, note=None):
    rows, chunk = prints.shape
    notes = [] if note is None else [note]
    rooms = [room + NOTE_ROWS * len(notes) for room in ROUND_ROWS]
    return pl.pallas_call(
        pack_body,
        grid=(chunk // WIDTH,),
        in_specs=[
            pl.BlockSpec((REACH + 1, STEP_TILES, rows), lambda step: (0, base + step, 0)),
            pl.BlockSpec((rows, WIDTH), lambda step: (0, step)),
        ]
        + [pl.BlockSpec((NOTE_ROWS, WIDTH), lambda step: (0, 0))] * len(notes),
        out_specs=[pl.BlockSpec((room, WIDTH), lambda step: (0, step)) for room in rooms],
        out_shape=[jax.ShapeDtypeStruct((room, chunk), jnp.bfloat16) for room in rooms],
        compiler_params=params(),
        cost_estimate=SMALL,
        name="pack",
    )(place, prints, *notes)


def pieces_in(lag, rows):
    size = PIECE_ROWS[lag]
    return [(piece, slice(piece * size, (piece + 1) * size)) for piece in range(rows // size)]


def multiply(flux_ref, part, sums_ref, piece):
    sums_ref[piece] += lax.dot_general(
        flux_ref[...], part, (((1,), (1,)), ((), ())), preferred_element_type=jnp.float32
    )


def finish(hour, obs_of, sums, samples, obs):
    samples_hours, size = sums.shape
    hours = samples_hours // samples
    row_hour = lax.rem(lax.broadcasted_iota(jnp.int32, (samples_hours, size), 0), hours)
    picked = jnp.sum(jnp.where(hour == row_hour, sums, 0.0).reshape(samples, hours, size), axis=1)
    to_obs = jnp.where(lax.broadcasted_iota(jnp.int32, (size, obs), 1) == obs_of, 1.0, 0.0)
    return jnp.dot(picked, to_obs, precision=lax.Precision.HIGHEST, preferred_element_type=jnp.float32)


def restore_body(lags, base, counts_ref, flux_ref, *refs):
    source_refs = refs[: len(lags)]
    place_ref, cols_ref, facts_ref = refs[len(lags) : len(lags) + 3]
    scratch = refs[-len(lags) :]
    out_ref = refs[-len(lags) - 1]
    rows = cols_ref.shape[1]
    total = sum(len(pieces_in(lag, rows)) for lag in lags)
    kept_refs = list(refs[-len(lags) - 1 - total : -len(lags) - 1])
    step = pl.program_id(0)
    final = step == pl.num_programs(0) - 1
    samples, obs = out_ref.shape[1:]

    @pl.when(step == 0)
    def _():
        out_ref[...] = jnp.zeros_like(out_ref)

    turn = lax.rem(TILE - STEP_TILES * (base + step), TILE)
    for index, lag in enumerate(lags):
        source_ref, sums_ref = source_refs[index], scratch[index]
        room = source_ref.shape[0]
        for piece, span in pieces_in(lag, rows):
            kept_ref = kept_refs.pop(0)
            size = kept_ref.shape[0]

            @pl.when(piece < counts_ref[lag])
            def _(lag=lag, index=index, piece=piece, span=span, kept_ref=kept_ref, size=size, room=room,
                  source_ref=source_ref, sums_ref=sums_ref):
                if lag == 0:
                    slots = lax.broadcasted_iota(jnp.int32, (size, room), 0) + span.start
                else:
                    places = pltpu.roll(cols_ref[index, span, :], turn, 1)
                    slots = lax.broadcasted_iota(jnp.int32, (size, room), 1)
                for tile in range(STEP_TILES):
                    cells = slice(tile * TILE, (tile + 1) * TILE)
                    place = place_ref[0, tile : tile + 1, :] if lag == 0 else places[:, tile : tile + 1]
                    back = product(one_hot(slots, place), source_ref[:, cells])
                    kept_ref[:, cells] = back.astype(jnp.bfloat16)

                @pl.when(step == 0)
                def _():
                    sums_ref[piece] = jnp.zeros(sums_ref.shape[1:], jnp.float32)

                multiply(flux_ref, kept_ref[...], sums_ref, piece)

                @pl.when(final)
                def _():
                    hour, obs_of = facts_ref[index, 6:7, span], cols_ref[index, span, :][:, -1:]
                    out_ref[index] += finish(hour, obs_of, sums_ref[piece], samples, obs)


def restore(lags, counts, flux, sources, place, cols, facts, samples, obs, base, kept):
    rows = cols.shape[1]
    cells, chunk = flux.shape[1], sources[0].shape[1]
    inputs = [flux, *sources, place, cols, facts]
    in_specs = (
        [pl.BlockSpec((flux.shape[0], WIDTH), lambda step, _: (0, base + step))]
        + [
            pl.BlockSpec((rows if lag == 0 else ROUND_ROWS[lag - 1], WIDTH), lambda step, _: (0, step)) for lag in lags
        ]
        + [
            pl.BlockSpec((1, STEP_TILES, rows), lambda step, _: (0, base + step, 0)),
            pl.BlockSpec(cols.shape, lambda step, _: (0, 0, 0)),
            pl.BlockSpec(facts.shape, lambda step, _: (0, 0, 0)),
        ]
    )
    pieces = [(lag, piece) for lag in lags for piece, _ in pieces_in(lag, rows)]
    aliases = {}
    if kept is not None:
        aliases = {1 + len(inputs) + index: index for index in range(len(pieces))}
        inputs += kept
        in_specs += [pl.BlockSpec(memory_space=pl.ANY)] * len(pieces)

    def kept_spec(lag, piece):
        return pl.BlockSpec(
            (PIECE_ROWS[lag], WIDTH), lambda step, counts: (0, jnp.where(piece < counts[lag], base + step, base))
        )

    def kernel(*refs):
        restore_body(lags, base, *refs)

    *kept, partial = pl.pallas_call(
        kernel,
        grid_spec=pltpu.PrefetchScalarGridSpec(
            num_scalar_prefetch=1,
            grid=(chunk // WIDTH,),
            in_specs=in_specs,
            out_specs=[kept_spec(lag, piece) for lag, piece in pieces]
            + [pl.BlockSpec((len(lags), samples, obs), lambda step, _: (0, 0, 0))],
            scratch_shapes=[
                pltpu.VMEM((rows // PIECE_ROWS[lag], flux.shape[0], PIECE_ROWS[lag]), jnp.float32) for lag in lags
            ],
        ),
        out_shape=[jax.ShapeDtypeStruct((PIECE_ROWS[lag], cells), jnp.bfloat16) for lag, _ in pieces]
        + [jax.ShapeDtypeStruct((len(lags), samples, obs), jnp.float32)],
        input_output_aliases=aliases,
        compiler_params=params(),
        cost_estimate=SMALL,
        name="restore",
    )(counts, *inputs)
    return kept, partial


def describe_body(blocks_ref, first_ref, note_ref, cols_ref, facts_ref):
    tiles = note_ref.shape[1] - 8
    obs, rows = note_ref.shape[2], cols_ref.shape[1]
    bands = rows // obs
    hours = first_ref[1]
    inside = jnp.concatenate([note_ref[0, tiles + band : tiles + band + 1, :] for band in range(bands)], axis=1)
    inside = inside - first_ref[0]
    coming = (inside >= 0) & (inside < hours)
    ones = jnp.where(coming, 1.0, 0.0)
    split = jnp.concatenate([ones[:, at : at + TILE] for at in range(0, rows, TILE)], axis=0)
    down = lax.broadcasted_iota(jnp.int32, (TILE, TILE), 0)
    ahead = jnp.where(down < lax.broadcasted_iota(jnp.int32, (TILE, TILE), 1), 1.0, 0.0).astype(jnp.bfloat16)
    within = product(split.astype(jnp.bfloat16), ahead)
    totals = jnp.sum(split, axis=1, keepdims=True)
    ranks, carried = [], jnp.zeros((1, 1), jnp.float32)
    for index in range(rows // TILE):
        ranks.append(within[index : index + 1, :] + carried)
        carried = carried + totals[index : index + 1, :]
    rank = jnp.where(coming, jnp.concatenate(ranks, axis=1), -1.0).astype(jnp.int32)
    hour = jnp.where(coming, inside, 0).astype(jnp.float32)
    obs_of = lax.rem(lax.broadcasted_iota(jnp.int32, (1, rows), 1), obs).astype(jnp.float32)
    on = note_ref[0, :tiles, :].astype(jnp.float32)
    table = jnp.concatenate(
        [jnp.concatenate([on] * bands, axis=1), jnp.zeros((TILE - tiles - 2, rows), jnp.float32), hour, obs_of], axis=0
    ).astype(jnp.bfloat16)
    size = PIECE_ROWS[0]
    below = lax.broadcasted_iota(jnp.int32, (size, size), 1) < lax.broadcasted_iota(jnp.int32, (size, size), 0)
    below = jnp.where(below, 1.0, 0.0).astype(jnp.bfloat16)
    lane = lax.broadcasted_iota(jnp.int32, (size, TILE), 1)
    both = (((1,), (1,)), ((), ()))
    sofar = jnp.zeros((1, TILE), jnp.float32)
    for piece in range(rows // size):
        span = slice(piece * size, (piece + 1) * size)
        sorter = one_hot(lax.broadcasted_iota(jnp.int32, (size, rows), 0) + span.start, rank)
        found = lax.dot_general(sorter, table, both, preferred_element_type=jnp.float32)
        place = product(below, found.astype(jnp.bfloat16)) + sofar
        sofar = sofar + jnp.sum(found, axis=0, keepdims=True)
        cols_ref[0, span, :] = jnp.where(lane < tiles, jnp.where(found > 0.0, place, -1.0), found).astype(jnp.int32)
        flat = lax.dot_general(table[TILE - 16 :], sorter, both, preferred_element_type=jnp.float32)
        facts_ref[0, :, span] = flat[8:].astype(jnp.int32)


def describe(first, notes, rows):
    count, height, obs = notes.shape
    return pl.pallas_call(
        describe_body,
        grid_spec=pltpu.PrefetchScalarGridSpec(
            num_scalar_prefetch=2,
            grid=(count,),
            in_specs=[pl.BlockSpec((1, height, obs), lambda step, *_: (step, 0, 0))],
            out_specs=[
                pl.BlockSpec((1, rows, TILE), lambda step, *_: (step, 0, 0)),
                pl.BlockSpec((1, 8, rows), lambda step, *_: (step, 0, 0)),
            ],
        ),
        out_shape=[
            jax.ShapeDtypeStruct((count, rows, TILE), jnp.int32),
            jax.ShapeDtypeStruct((count, 8, rows), jnp.int32),
        ],
        compiler_params=params(),
        cost_estimate=SMALL,
        name="describe",
    )(first, first, notes)


def adjoint_body(counts_ref, *refs):
    count = REACH + 1
    residual_refs, own_facts_ref, facts_ref = refs[:count], refs[count], refs[count + 1]
    spread_refs, out_ref = refs[-count:], refs[-count - 1]
    kept_refs = refs[count + 2 : -count - 1]
    rows = facts_ref.shape[2]
    samples, obs = residual_refs[0].shape
    samples_hours = out_ref.shape[0]
    hours = samples_hours // samples
    pieces = [(lag, piece, span) for lag in range(count) for piece, span in pieces_in(lag, rows)]

    @pl.when(pl.program_id(0) == 0)
    def _():
        for lag, piece, span in pieces:

            @pl.when(piece < counts_ref[lag])
            def _(lag=lag, piece=piece, span=span):
                size = span.stop - span.start
                slots = lax.broadcasted_iota(jnp.int32, (obs, size), 0)
                its_hour = own_facts_ref[0, 6:7, span] if lag == 0 else facts_ref[lag - 1, 6:7, span]
                its_obs = own_facts_ref[0, 7:8, span] if lag == 0 else facts_ref[lag - 1, 7:8, span]
                value = product(residual_refs[lag][...], one_hot(slots, its_obs))
                value = jnp.broadcast_to(value[:, None, :], (samples, hours, size))
                row_hour = lax.broadcasted_iota(jnp.int32, (samples, hours, size), 1)
                spread = jnp.where(its_hour[None] == row_hour, value, 0.0).reshape(samples_hours, size)
                spread_refs[lag][piece] = spread.astype(jnp.bfloat16)

    total = None
    for index, (lag, piece, _) in enumerate(pieces):
        if piece == 0:
            term = product(spread_refs[lag][0], kept_refs[index][...])
            total = term if total is None else total + term
    out_ref[...] = total
    for index, (lag, piece, _) in enumerate(pieces):
        if piece > 0:

            @pl.when(piece < counts_ref[lag])
            def _(index=index, lag=lag, piece=piece):
                out_ref[...] += product(spread_refs[lag][piece], kept_refs[index][...])


def adjoint(counts, residuals, own_facts, facts, kept, samples_hours, width=512):
    rows, cells = facts.shape[2], kept[0].shape[1]
    count = REACH + 1
    pieces = [(lag, piece) for lag in range(count) for piece, _ in pieces_in(lag, rows)]

    def kept_spec(lag, piece):
        return pl.BlockSpec(
            (PIECE_ROWS[lag], width), lambda step, counts: (0, jnp.where(piece < counts[lag], step, 0))
        )

    return pl.pallas_call(
        adjoint_body,
        grid_spec=pltpu.PrefetchScalarGridSpec(
            num_scalar_prefetch=1,
            grid=(cells // width,),
            in_specs=[pl.BlockSpec(residuals[0].shape, lambda step, _: (0, 0))] * count
            + [pl.BlockSpec(part.shape, lambda step, _: (0, 0, 0)) for part in (own_facts, facts)]
            + [kept_spec(lag, piece) for lag, piece in pieces],
            out_specs=pl.BlockSpec((samples_hours, width), lambda step, _: (0, step)),
            scratch_shapes=[
                pltpu.VMEM((rows // size, samples_hours, size), jnp.bfloat16) for size in PIECE_ROWS
            ],
        ),
        out_shape=jax.ShapeDtypeStruct((samples_hours, cells), jnp.float32),
        compiler_params=params(),
        cost_estimate=SMALL,
        name="adjoint",
    )(counts, *residuals, own_facts, facts, *kept)


def body(flux, footprint, band_lag, obs_hour, tile_mask, obs_value, obs_weight):
    samples, hours, cells = flux.shape
    obs, bands, _ = footprint.shape
    tiles = tile_mask.shape[1]
    rows = bands * obs
    position = lax.axis_index("tm")
    flux_rows = flux.reshape(samples * hours, cells)

    source = (obs_hour[:, None] - band_lag).T
    mask = tile_mask.T
    blank = jnp.zeros((8 - bands, obs), jnp.int32)
    note = jnp.concatenate([mask, source, blank], axis=0)
    carried = jnp.concatenate(
        [mask[at : at + NOTE_ROWS] for at in range(0, tiles, NOTE_ROWS)]
        + [jnp.concatenate([source - position * hours, jnp.zeros((NOTE_ROWS - bands, obs), jnp.int32)], axis=0)],
        axis=1,
    )
    carried = jnp.pad(carried, ((0, 0), (0, WIDTH - carried.shape[1]))).astype(jnp.bfloat16)

    def hour_in(hour, block):
        inside = hour - block * hours
        return jnp.where((inside >= 0) & (inside < hours), inside, -1).reshape(rows)

    down = lax.broadcasted_iota(jnp.int32, (rows, rows), 0)
    along = lax.broadcasted_iota(jnp.int32, (rows, rows), 1)
    before = (down < along).astype(jnp.bfloat16)

    to_block = jnp.stack([hour_in(source, position - lag) >= 0 for lag in range(REACH + 1)])
    on = jnp.tile(mask, (1, bands)) > 0
    leaving = to_block[:, None, :] & on[None]
    ranked = jnp.concatenate([jnp.broadcast_to(to_block[:1, None, :], (1, tiles, rows)), leaving[1:]], axis=0)
    place = lax.dot_general(
        ranked.astype(jnp.bfloat16), before, (((2,), (0,)), ((), ())), preferred_element_type=jnp.float32
    )
    place = jnp.where(leaving, place.astype(jnp.int32), -1)
    counts = jnp.max(jnp.sum(leaving[1:].astype(jnp.int32), axis=2), axis=1)
    room = jnp.array(ROUND_ROWS, jnp.int32)
    need = jnp.max((counts + room - 1) // room)

    starts = [sum(CHUNK_STEPS[:chunk]) for chunk in range(len(CHUNK_STEPS))]

    def prints_of(chunk, footprint):
        first, last = starts[chunk] * WIDTH, (starts[chunk] + CHUNK_STEPS[chunk]) * WIDTH
        return footprint[:, :, first:last].transpose(1, 0, 2).reshape(rows, last - first)

    chunks = range(len(CHUNK_STEPS))
    prints, packs, moved = [], [], []
    for chunk in chunks:
        if packs:
            footprint, packs[-1] = lax.optimization_barrier((footprint, packs[-1]))
        prints.append(prints_of(chunk, footprint))
        packs.append(pack(place, prints[chunk], starts[chunk], None if chunk else carried))
    for chunk in chunks:
        moved.append([shifted(part, -lag - 1) for lag, part in enumerate(packs[chunk][:-1])])
        third, passing = shifted_three(packs[chunk][-1])
        moved[chunk].append(third)

    first = jnp.stack([position * hours, jnp.int32(hours)])
    def counts_of(parts):
        hour = jnp.stack([hour_in(part[tiles : tiles + bands], position) for part in parts])
        sizes = jnp.array(PIECE_ROWS[: len(parts)], jnp.int32)
        return jnp.maximum((jnp.sum((hour >= 0).astype(jnp.int32), axis=1) + sizes - 1) // sizes, 1)

    own_note, _ = lax.optimization_barrier((note, passing))
    own_count = counts_of([own_note])
    own_cols, own_facts = describe(first, own_note[None], rows)

    own, own_partial = None, 0.0
    for chunk in chunks:
        own, part = restore(
            (0,), own_count, flux_rows, [prints[chunk]], place, own_cols, own_facts, samples, obs, starts[chunk], own
        )
        own_partial = own_partial + part[0]
    need, own[0] = lax.optimization_barrier((need, own[0]))
    everyone = lax.axis_size("tm") * lax.axis_size("cells")
    needs = jnp.broadcast_to(need, (everyone, TILE))
    rounds = jnp.max(lax.all_to_all(needs, ("tm", "cells"), 0, 0, tiled=True))

    *moved[0], own_partial = lax.optimization_barrier((*moved[0], own_partial))
    notes = []
    for lag, part in enumerate(moved[0]):
        came = part[ROUND_ROWS[lag] :].astype(jnp.int32)
        parts = [came[:, at : at + obs] for at in range(0, (tiles // NOTE_ROWS + 1) * obs, obs)]
        parts[-1] = parts[-1][:bands] + (position + lag + 1) * hours
        notes.append(jnp.concatenate(parts + [blank], axis=0))
    cols, facts = describe(first, jnp.stack(notes), rows)
    counts = counts_of([note] + list(notes))

    def restore_all(arrived, cols):
        total, kept = 0.0, None
        for chunk in chunks:
            kept, part = restore(
                tuple(range(1, REACH + 1)), counts, flux_rows, arrived[chunk], place, cols, facts, samples, obs,
                starts[chunk], kept,
            )
            total = total + part
        return kept, total

    state = restore_all(moved, cols)

    def further(index, state):
        lower = index * jnp.concatenate([jnp.zeros((1,), jnp.int32), room])
        arrived = []
        for chunk in chunks:
            packed = pack(place - lower[:, None, None], prints[chunk], starts[chunk], None if chunk else carried)
            arrived.append([shifted(part, -lag - 1) for lag, part in enumerate(packed)])
        lane = lax.broadcasted_iota(jnp.int32, cols.shape, 2)
        more, added = restore_all(arrived, jnp.where(lane < tiles, cols - lower[1:, None, None], cols))
        kept, total = state
        return [a + b for a, b in zip(kept, more)], total + added

    kept, total = lax.fori_loop(1, rounds, further, state)

    column = position % WRAP
    cores = lax.axis_size("cells")
    by_lag = jnp.concatenate([own_partial[None], total] * 2)
    slots = lax.dynamic_slice_in_dim(by_lag, (WRAP - column) % WRAP, WRAP)
    group = WRAP * cores
    rows_of_chips = [list(range(at, at + group)) for at in range(0, everyone, group)]
    sums = lax.all_to_all(
        jnp.repeat(slots, cores, axis=0), ("tm", "cells"), 0, 0, axis_index_groups=rows_of_chips, tiled=True
    )
    sums = jnp.sum(sums.reshape(WRAP, cores, samples, obs), axis=1)
    here = (jnp.arange(WRAP) <= column)[:, None, None]
    across = jnp.sum(jnp.where(here, 0.0, sums), axis=0)
    modeled = jnp.sum(jnp.where(here, sums, 0.0), axis=0) + shifted(across, WRAP)
    residual = (obs_weight[None, :] * (modeled - obs_value)).astype(jnp.bfloat16)
    above = shifted(residual, -WRAP)
    slots = jnp.where(here, residual[None], above[None])
    lines = [list(range(at, at + WRAP)) for at in range(0, lax.axis_size("tm"), WRAP)]
    shared = lax.all_to_all(slots, "tm", 0, 0, axis_index_groups=lines, tiled=True)
    shared = lax.dynamic_slice_in_dim(jnp.concatenate([shared] * 2), column, WRAP)
    residuals = [shared[lag] for lag in range(REACH + 1)]
    gradient = adjoint(counts, residuals, own_facts, facts, own + list(kept), samples * hours)
    return modeled, gradient.reshape(samples, hours, cells)


def solution(mesh):
    placed = (
        P(None, "tm", "cells"),
        P("tm", None, "cells"),
        P("tm", None),
        P("tm"),
        P("tm", "cells"),
        P(None, "tm"),
        P("tm"),
    )
    return jax.shard_map(
        body,
        mesh=mesh,
        in_specs=placed,
        out_specs=(P(None, "tm"), P(None, "tm", "cells")),
        check_vma=False,
    )
```

```python
import jax
import jax.numpy as jnp
from jax import lax
from jax.experimental import pallas as pl
from jax.experimental.pallas import tpu as pltpu
from jax.sharding import PartitionSpec as P

REACH = 3
TILE = 128
STEP_TILES = 8
WIDTH = STEP_TILES * TILE
ROUND_ROWS = (256, 256, 128)
NOTE_ROWS = 16
PIECE_ROWS = (256, 512, 512, 256)
SMALL = pl.CostEstimate(flops=1000, bytes_accessed=1000, transcendentals=0)
CHUNK_STEPS = (2, 2)
VMEM_BYTES = 48 * 1024 * 1024
WRAP = 4


def shifted(value, steps):
    count = lax.axis_size("tm")
    initial, last = (max(0, -steps), min(count, count - steps))
    return lax.ppermute(value, "tm", [(source, source + steps) for source in range(initial, last)])


def swapped(value):
    return lax.ppermute(value, "cells", [(0, 1), (1, 0)])


def shifted_three(value):
    count = lax.axis_size("tm")
    turned = WRAP - 1
    up = [(source, source - WRAP) for source in range(WRAP, count) if source % WRAP != turned]
    above = lax.ppermute(value, "tm", up)
    there = jnp.where(lax.axis_index("tm") % WRAP == turned, value, above)
    ring = [(source, source - source % WRAP + (source + 1) % WRAP) for source in range(count)]
    return lax.ppermute(there, "tm", ring), above


def params():
    return pltpu.CompilerParams(vmem_limit_bytes=VMEM_BYTES)


def one_hot(wanted, position):
    return jnp.where(wanted == position, 1.0, 0.0).astype(jnp.bfloat16)


def product(left, right):
    return jnp.dot(left, right, preferred_element_type=jnp.float32)


def pack_body(place_ref, prints_ref, *refs):
    rows = prints_ref.shape[0]
    out_refs = refs[-REACH:]
    for room, out_ref in zip(ROUND_ROWS, out_refs):
        if len(refs) > REACH:
            out_ref[room:, :] = refs[0][...]
    for tile in range(STEP_TILES):
        cells = slice(tile * TILE, (tile + 1) * TILE)
        for lag, out_ref in enumerate(out_refs):
            place = place_ref[lag + 1, tile : tile + 1, :]
            room = ROUND_ROWS[lag]
            slots = lax.broadcasted_iota(jnp.int32, (room, rows), 0)
            out_ref[:room, cells] = product(one_hot(slots, place), prints_ref[:, cells]).astype(jnp.bfloat16)


def pack(place, prints, base, note=None):
    rows, chunk = prints.shape
    notes = [] if note is None else [note]
    rooms = [room + NOTE_ROWS * len(notes) for room in ROUND_ROWS]
    return pl.pallas_call(
        pack_body,
        grid=(chunk // WIDTH,),
        in_specs=[
            pl.BlockSpec((REACH + 1, STEP_TILES, rows), lambda step: (0, base + step, 0)),
            pl.BlockSpec((rows, WIDTH), lambda step: (0, step)),
        ]
        + [pl.BlockSpec((NOTE_ROWS, WIDTH), lambda step: (0, 0))] * len(notes),
        out_specs=[pl.BlockSpec((room, WIDTH), lambda step: (0, step)) for room in rooms],
        out_shape=[jax.ShapeDtypeStruct((room, chunk), jnp.bfloat16) for room in rooms],
        compiler_params=params(),
        cost_estimate=SMALL,
        name="pack",
    )(place, prints, *notes)


def pieces_in(lag, rows):
    size = PIECE_ROWS[lag]
    return [(piece, slice(piece * size, (piece + 1) * size)) for piece in range(rows // size)]


def multiply(flux_ref, part, sums_ref, piece):
    sums_ref[piece] += lax.dot_general(
        flux_ref[...], part, (((1,), (1,)), ((), ())), preferred_element_type=jnp.float32
    )


def finish(hour, obs_of, sums, samples, obs):
    samples_hours, size = sums.shape
    hours = samples_hours // samples
    row_hour = lax.rem(lax.broadcasted_iota(jnp.int32, (samples_hours, size), 0), hours)
    picked = jnp.sum(jnp.where(hour == row_hour, sums, 0.0).reshape(samples, hours, size), axis=1)
    to_obs = jnp.where(lax.broadcasted_iota(jnp.int32, (size, obs), 1) == obs_of, 1.0, 0.0)
    return jnp.dot(picked, to_obs, precision=lax.Precision.HIGHEST, preferred_element_type=jnp.float32)


def restore_body(lags, base, counts_ref, flux_ref, *refs):
    source_refs = refs[: len(lags)]
    place_ref, cols_ref, facts_ref = refs[len(lags) : len(lags) + 3]
    scratch = refs[-len(lags) :]
    out_ref = refs[-len(lags) - 1]
    rows = cols_ref.shape[1]
    total = sum(len(pieces_in(lag, rows)) for lag in lags)
    kept_refs = list(refs[-len(lags) - 1 - total : -len(lags) - 1])
    step = pl.program_id(0)
    final = step == pl.num_programs(0) - 1
    samples, obs = out_ref.shape[1:]

    @pl.when(step == 0)
    def _():
        out_ref[...] = jnp.zeros_like(out_ref)

    turn = lax.rem(TILE - STEP_TILES * (base + step), TILE)
    for index, lag in enumerate(lags):
        source_ref, sums_ref = source_refs[index], scratch[index]
        room = source_ref.shape[0]
        for piece, span in pieces_in(lag, rows):
            kept_ref = kept_refs.pop(0)
            size = kept_ref.shape[0]

            @pl.when(piece < counts_ref[lag])
            def _(lag=lag, index=index, piece=piece, span=span, kept_ref=kept_ref, size=size, room=room,
                  source_ref=source_ref, sums_ref=sums_ref):
                if lag == 0:
                    slots = lax.broadcasted_iota(jnp.int32, (size, room), 0) + span.start
                else:
                    places = pltpu.roll(cols_ref[index, span, :], turn, 1)
                    slots = lax.broadcasted_iota(jnp.int32, (size, room), 1)
                for tile in range(STEP_TILES):
                    cells = slice(tile * TILE, (tile + 1) * TILE)
                    place = place_ref[0, tile : tile + 1, :] if lag == 0 else places[:, tile : tile + 1]
                    back = product(one_hot(slots, place), source_ref[:, cells])
                    kept_ref[:, cells] = back.astype(jnp.bfloat16)

                @pl.when(step == 0)
                def _():
                    sums_ref[piece] = jnp.zeros(sums_ref.shape[1:], jnp.float32)

                multiply(flux_ref, kept_ref[...], sums_ref, piece)

                @pl.when(final)
                def _():
                    hour, obs_of = facts_ref[index, 6:7, span], cols_ref[index, span, :][:, -1:]
                    out_ref[index] += finish(hour, obs_of, sums_ref[piece], samples, obs)


def restore(lags, counts, flux, sources, place, cols, facts, samples, obs, base, kept):
    rows = cols.shape[1]
    cells, chunk = flux.shape[1], sources[0].shape[1]
    inputs = [flux, *sources, place, cols, facts]
    in_specs = (
        [pl.BlockSpec((flux.shape[0], WIDTH), lambda step, _: (0, base + step))]
        + [
            pl.BlockSpec((rows if lag == 0 else ROUND_ROWS[lag - 1], WIDTH), lambda step, _: (0, step)) for lag in lags
        ]
        + [
            pl.BlockSpec((1, STEP_TILES, rows), lambda step, _: (0, base + step, 0)),
            pl.BlockSpec(cols.shape, lambda step, _: (0, 0, 0)),
            pl.BlockSpec(facts.shape, lambda step, _: (0, 0, 0)),
        ]
    )
    pieces = [(lag, piece) for lag in lags for piece, _ in pieces_in(lag, rows)]
    aliases = {}
    if kept is not None:
        aliases = {1 + len(inputs) + index: index for index in range(len(pieces))}
        inputs += kept
        in_specs += [pl.BlockSpec(memory_space=pl.ANY)] * len(pieces)

    def kept_spec(lag, piece):
        return pl.BlockSpec(
            (PIECE_ROWS[lag], WIDTH), lambda step, counts: (0, jnp.where(piece < counts[lag], base + step, base))
        )

    def kernel(*refs):
        restore_body(lags, base, *refs)

    *kept, partial = pl.pallas_call(
        kernel,
        grid_spec=pltpu.PrefetchScalarGridSpec(
            num_scalar_prefetch=1,
            grid=(chunk // WIDTH,),
            in_specs=in_specs,
            out_specs=[kept_spec(lag, piece) for lag, piece in pieces]
            + [pl.BlockSpec((len(lags), samples, obs), lambda step, _: (0, 0, 0))],
            scratch_shapes=[
                pltpu.VMEM((rows // PIECE_ROWS[lag], flux.shape[0], PIECE_ROWS[lag]), jnp.float32) for lag in lags
            ],
        ),
        out_shape=[jax.ShapeDtypeStruct((PIECE_ROWS[lag], cells), jnp.bfloat16) for lag, _ in pieces]
        + [jax.ShapeDtypeStruct((len(lags), samples, obs), jnp.float32)],
        input_output_aliases=aliases,
        compiler_params=params(),
        cost_estimate=SMALL,
        name="restore",
    )(counts, *inputs)
    return kept, partial


def describe_body(blocks_ref, first_ref, note_ref, cols_ref, facts_ref):
    tiles = note_ref.shape[1] - 8
    obs, rows = note_ref.shape[2], cols_ref.shape[1]
    bands = rows // obs
    hours = first_ref[1]
    inside = jnp.concatenate([note_ref[0, tiles + band : tiles + band + 1, :] for band in range(bands)], axis=1)
    inside = inside - first_ref[0]
    coming = (inside >= 0) & (inside < hours)
    ones = jnp.where(coming, 1.0, 0.0)
    split = jnp.concatenate([ones[:, at : at + TILE] for at in range(0, rows, TILE)], axis=0)
    down = lax.broadcasted_iota(jnp.int32, (TILE, TILE), 0)
    ahead = jnp.where(down < lax.broadcasted_iota(jnp.int32, (TILE, TILE), 1), 1.0, 0.0).astype(jnp.bfloat16)
    within = product(split.astype(jnp.bfloat16), ahead)
    totals = jnp.sum(split, axis=1, keepdims=True)
    ranks, carried = [], jnp.zeros((1, 1), jnp.float32)
    for index in range(rows // TILE):
        ranks.append(within[index : index + 1, :] + carried)
        carried = carried + totals[index : index + 1, :]
    rank = jnp.where(coming, jnp.concatenate(ranks, axis=1), -1.0).astype(jnp.int32)
    hour = jnp.where(coming, inside, 0).astype(jnp.float32)
    obs_of = lax.rem(lax.broadcasted_iota(jnp.int32, (1, rows), 1), obs).astype(jnp.float32)
    on = note_ref[0, :tiles, :].astype(jnp.float32)
    table = jnp.concatenate(
        [jnp.concatenate([on] * bands, axis=1), jnp.zeros((TILE - tiles - 2, rows), jnp.float32), hour, obs_of], axis=0
    ).astype(jnp.bfloat16)
    size = PIECE_ROWS[0]
    below = lax.broadcasted_iota(jnp.int32, (size, size), 1) < lax.broadcasted_iota(jnp.int32, (size, size), 0)
    below = jnp.where(below, 1.0, 0.0).astype(jnp.bfloat16)
    lane = lax.broadcasted_iota(jnp.int32, (size, TILE), 1)
    both = (((1,), (1,)), ((), ()))
    sofar = jnp.zeros((1, TILE), jnp.float32)
    for piece in range(rows // size):
        span = slice(piece * size, (piece + 1) * size)
        sorter = one_hot(lax.broadcasted_iota(jnp.int32, (size, rows), 0) + span.start, rank)
        found = lax.dot_general(sorter, table, both, preferred_element_type=jnp.float32)
        place = product(below, found.astype(jnp.bfloat16)) + sofar
        sofar = sofar + jnp.sum(found, axis=0, keepdims=True)
        cols_ref[0, span, :] = jnp.where(lane < tiles, jnp.where(found > 0.0, place, -1.0), found).astype(jnp.int32)
        flat = lax.dot_general(table[TILE - 16 :], sorter, both, preferred_element_type=jnp.float32)
        facts_ref[0, :, span] = flat[8:].astype(jnp.int32)


def describe(first, notes, rows):
    count, height, obs = notes.shape
    return pl.pallas_call(
        describe_body,
        grid_spec=pltpu.PrefetchScalarGridSpec(
            num_scalar_prefetch=2,
            grid=(count,),
            in_specs=[pl.BlockSpec((1, height, obs), lambda step, *_: (step, 0, 0))],
            out_specs=[
                pl.BlockSpec((1, rows, TILE), lambda step, *_: (step, 0, 0)),
                pl.BlockSpec((1, 8, rows), lambda step, *_: (step, 0, 0)),
            ],
        ),
        out_shape=[
            jax.ShapeDtypeStruct((count, rows, TILE), jnp.int32),
            jax.ShapeDtypeStruct((count, 8, rows), jnp.int32),
        ],
        compiler_params=params(),
        cost_estimate=SMALL,
        name="describe",
    )(first, first, notes)


def adjoint_body(counts_ref, *refs):
    count = REACH + 1
    residual_refs, own_facts_ref, facts_ref = refs[:count], refs[count], refs[count + 1]
    spread_refs, out_ref = refs[-count:], refs[-count - 1]
    kept_refs = refs[count + 2 : -count - 1]
    rows = facts_ref.shape[2]
    samples, obs = residual_refs[0].shape
    samples_hours = out_ref.shape[0]
    hours = samples_hours // samples
    pieces = [(lag, piece, span) for lag in range(count) for piece, span in pieces_in(lag, rows)]

    @pl.when(pl.program_id(0) == 0)
    def _():
        for lag, piece, span in pieces:

            @pl.when(piece < counts_ref[lag])
            def _(lag=lag, piece=piece, span=span):
                size = span.stop - span.start
                slots = lax.broadcasted_iota(jnp.int32, (obs, size), 0)
                its_hour = own_facts_ref[0, 6:7, span] if lag == 0 else facts_ref[lag - 1, 6:7, span]
                its_obs = own_facts_ref[0, 7:8, span] if lag == 0 else facts_ref[lag - 1, 7:8, span]
                value = product(residual_refs[lag][...], one_hot(slots, its_obs))
                value = jnp.broadcast_to(value[:, None, :], (samples, hours, size))
                row_hour = lax.broadcasted_iota(jnp.int32, (samples, hours, size), 1)
                spread = jnp.where(its_hour[None] == row_hour, value, 0.0).reshape(samples_hours, size)
                spread_refs[lag][piece] = spread.astype(jnp.bfloat16)

    total = None
    for index, (lag, piece, _) in enumerate(pieces):
        if piece == 0:
            term = product(spread_refs[lag][0], kept_refs[index][...])
            total = term if total is None else total + term
    out_ref[...] = total
    for index, (lag, piece, _) in enumerate(pieces):
        if piece > 0:

            @pl.when(piece < counts_ref[lag])
            def _(index=index, lag=lag, piece=piece):
                out_ref[...] += product(spread_refs[lag][piece], kept_refs[index][...])


def adjoint(counts, residuals, own_facts, facts, kept, samples_hours, width=512):
    rows, cells = facts.shape[2], kept[0].shape[1]
    count = REACH + 1
    pieces = [(lag, piece) for lag in range(count) for piece, _ in pieces_in(lag, rows)]

    def kept_spec(lag, piece):
        return pl.BlockSpec(
            (PIECE_ROWS[lag], width), lambda step, counts: (0, jnp.where(piece < counts[lag], step, 0))
        )

    return pl.pallas_call(
        adjoint_body,
        grid_spec=pltpu.PrefetchScalarGridSpec(
            num_scalar_prefetch=1,
            grid=(cells // width,),
            in_specs=[pl.BlockSpec(residuals[0].shape, lambda step, _: (0, 0))] * count
            + [pl.BlockSpec(part.shape, lambda step, _: (0, 0, 0)) for part in (own_facts, facts)]
            + [kept_spec(lag, piece) for lag, piece in pieces],
            out_specs=pl.BlockSpec((samples_hours, width), lambda step, _: (0, step)),
            scratch_shapes=[
                pltpu.VMEM((rows // size, samples_hours, size), jnp.bfloat16) for size in PIECE_ROWS
            ],
        ),
        out_shape=jax.ShapeDtypeStruct((samples_hours, cells), jnp.float32),
        compiler_params=params(),
        cost_estimate=SMALL,
        name="adjoint",
    )(counts, *residuals, own_facts, facts, *kept)


def body(flux, footprint, band_lag, obs_hour, tile_mask, obs_value, obs_weight):
    samples, hours, cells = flux.shape
    obs, bands, _ = footprint.shape
    tiles = tile_mask.shape[1]
    rows = bands * obs
    position = lax.axis_index("tm")
    flux_rows = flux.reshape(samples * hours, cells)

    source = (obs_hour[:, None] - band_lag).T
    mask = tile_mask.T
    blank = jnp.zeros((8 - bands, obs), jnp.int32)
    note = jnp.concatenate([mask, source, blank], axis=0)
    carried = jnp.concatenate(
        [mask[at : at + NOTE_ROWS] for at in range(0, tiles, NOTE_ROWS)]
        + [jnp.concatenate([source - position * hours, jnp.zeros((NOTE_ROWS - bands, obs), jnp.int32)], axis=0)],
        axis=1,
    )
    carried = jnp.pad(carried, ((0, 0), (0, WIDTH - carried.shape[1]))).astype(jnp.bfloat16)

    def hour_in(hour, block):
        inside = hour - block * hours
        return jnp.where((inside >= 0) & (inside < hours), inside, -1).reshape(rows)

    down = lax.broadcasted_iota(jnp.int32, (rows, rows), 0)
    along = lax.broadcasted_iota(jnp.int32, (rows, rows), 1)
    before = (down < along).astype(jnp.bfloat16)

    to_block = jnp.stack([hour_in(source, position - lag) >= 0 for lag in range(REACH + 1)])
    on = jnp.tile(mask, (1, bands)) > 0
    leaving = to_block[:, None, :] & on[None]
    ranked = jnp.concatenate([jnp.broadcast_to(to_block[:1, None, :], (1, tiles, rows)), leaving[1:]], axis=0)
    place = lax.dot_general(
        ranked.astype(jnp.bfloat16), before, (((2,), (0,)), ((), ())), preferred_element_type=jnp.float32
    )
    place = jnp.where(leaving, place.astype(jnp.int32), -1)
    counts = jnp.max(jnp.sum(leaving[1:].astype(jnp.int32), axis=2), axis=1)
    room = jnp.array(ROUND_ROWS, jnp.int32)
    need = jnp.max((counts + room - 1) // room)

    starts = [sum(CHUNK_STEPS[:chunk]) for chunk in range(len(CHUNK_STEPS))]

    def prints_of(chunk, footprint):
        first, last = starts[chunk] * WIDTH, (starts[chunk] + CHUNK_STEPS[chunk]) * WIDTH
        return footprint[:, :, first:last].transpose(1, 0, 2).reshape(rows, last - first)

    chunks = range(len(CHUNK_STEPS))
    prints, packs, moved = [], [], []
    for chunk in chunks:
        if packs:
            footprint, packs[-1] = lax.optimization_barrier((footprint, packs[-1]))
        prints.append(prints_of(chunk, footprint))
        packs.append(pack(place, prints[chunk], starts[chunk], None if chunk else carried))
    for chunk in chunks:
        moved.append([shifted(part, -lag - 1) for lag, part in enumerate(packs[chunk][:-1])])
        third, passing = shifted_three(packs[chunk][-1])
        moved[chunk].append(third)

    first = jnp.stack([position * hours, jnp.int32(hours)])
    def counts_of(parts):
        hour = jnp.stack([hour_in(part[tiles : tiles + bands], position) for part in parts])
        sizes = jnp.array(PIECE_ROWS[: len(parts)], jnp.int32)
        return jnp.maximum((jnp.sum((hour >= 0).astype(jnp.int32), axis=1) + sizes - 1) // sizes, 1)

    own_note, _ = lax.optimization_barrier((note, passing))
    own_count = counts_of([own_note])
    own_cols, own_facts = describe(first, own_note[None], rows)

    own, own_partial = None, 0.0
    for chunk in chunks:
        own, part = restore(
            (0,), own_count, flux_rows, [prints[chunk]], place, own_cols, own_facts, samples, obs, starts[chunk], own
        )
        own_partial = own_partial + part[0]
    *moved[0], own_partial = lax.optimization_barrier((*moved[0], own_partial))
    notes = []
    for lag, part in enumerate(moved[0]):
        came = part[ROUND_ROWS[lag] :].astype(jnp.int32)
        parts = [came[:, at : at + obs] for at in range(0, (tiles // NOTE_ROWS + 1) * obs, obs)]
        parts[-1] = parts[-1][:bands] + (position + lag + 1) * hours
        notes.append(jnp.concatenate(parts + [blank], axis=0))
    cols, facts = describe(first, jnp.stack(notes), rows)
    counts = counts_of([note] + list(notes))

    def restore_chunk(chunk, arrived, cols, kept):
        return restore(
            tuple(range(1, REACH + 1)), counts, flux_rows, arrived, place, cols, facts, samples, obs, starts[chunk], kept
        )

    kept, total = restore_chunk(0, moved[0], cols, None)
    need, total = lax.optimization_barrier((need, total))
    everyone = lax.axis_size("tm") * lax.axis_size("cells")
    needs = jnp.broadcast_to(need, (everyone, TILE))
    rounds = jnp.max(lax.all_to_all(needs, ("tm", "cells"), 0, 0, tiled=True))
    for chunk in chunks[1:]:
        kept, part = restore_chunk(chunk, moved[chunk], cols, kept)
        total = total + part

    def further(index, state):
        lower = index * jnp.concatenate([jnp.zeros((1,), jnp.int32), room])
        arrived = []
        for chunk in chunks:
            packed = pack(place - lower[:, None, None], prints[chunk], starts[chunk], None if chunk else carried)
            arrived.append([shifted(part, -lag - 1) for lag, part in enumerate(packed)])
        lane = lax.broadcasted_iota(jnp.int32, cols.shape, 2)
        lowered = jnp.where(lane < tiles, cols - lower[1:, None, None], cols)
        more, added = None, 0.0
        for chunk in chunks:
            more, part = restore_chunk(chunk, arrived[chunk], lowered, more)
            added = added + part
        kept, total = state
        return [a + b for a, b in zip(kept, more)], total + added

    kept, total = lax.fori_loop(1, rounds, further, (kept, total))

    column = position % WRAP
    cores = lax.axis_size("cells")
    by_lag = jnp.concatenate([own_partial[None], total] * 2)
    slots = lax.dynamic_slice_in_dim(by_lag, (WRAP - column) % WRAP, WRAP)
    group = WRAP * cores
    rows_of_chips = [list(range(at, at + group)) for at in range(0, everyone, group)]
    sums = lax.all_to_all(
        jnp.repeat(slots, cores, axis=0), ("tm", "cells"), 0, 0, axis_index_groups=rows_of_chips, tiled=True
    )
    sums = jnp.sum(sums.reshape(WRAP, cores, samples, obs), axis=1)
    here = (jnp.arange(WRAP) <= column)[:, None, None]
    across = jnp.sum(jnp.where(here, 0.0, sums), axis=0)
    modeled = jnp.sum(jnp.where(here, sums, 0.0), axis=0) + shifted(across, WRAP)
    residual = (obs_weight[None, :] * (modeled - obs_value)).astype(jnp.bfloat16)
    above = shifted(residual, -WRAP)
    slots = jnp.where(here, residual[None], above[None])
    lines = [list(range(at, at + WRAP)) for at in range(0, lax.axis_size("tm"), WRAP)]
    shared = lax.all_to_all(slots, "tm", 0, 0, axis_index_groups=lines, tiled=True)
    shared = lax.dynamic_slice_in_dim(jnp.concatenate([shared] * 2), column, WRAP)
    residuals = [shared[lag] for lag in range(REACH + 1)]
    gradient = adjoint(counts, residuals, own_facts, facts, own + list(kept), samples * hours)
    return modeled, gradient.reshape(samples, hours, cells)


def solution(mesh):
    placed = (
        P(None, "tm", "cells"),
        P("tm", None, "cells"),
        P("tm", None),
        P("tm"),
        P("tm", "cells"),
        P(None, "tm"),
        P("tm"),
    )
    return jax.shard_map(
        body,
        mesh=mesh,
        in_specs=placed,
        out_specs=(P(None, "tm"), P(None, "tm", "cells")),
        check_vma=False,
    )
```
